256 devices in a mesh: grp: 8 (over z_lo, x), ep: 32 (over y, z_hi, core).
Axes of the slice: x: 4, y: 4, z: 8 (z_hi: 4, z_lo: 2; z = z_hi * 2 + z_lo), core: 2. Of those that a mesh axis runs over, the one named last changes fastest.
Arguments:
- tokens_one: bfloat16 [8192, 2048], P(('grp', 'ep')), may hold values from -6 to 6
- routes_one: int32 [8192, 6], P(('grp', 'ep')), may hold values from 0 to 31, all different within a row; in each aligned block of 32 rows (0 to 31, 32 to 63, ...) at most 9 rows name the same one
- gates_one: bfloat16 [8192, 6], P(('grp', 'ep')), may hold values from 0.049804688 to 0.3984375
- tokens_two: bfloat16 [8192, 2048], P(('grp', 'ep')), may hold values from -6 to 6
- routes_two: int32 [8192, 6], P(('grp', 'ep')), may hold values from 0 to 31, all different within a row; in each aligned block of 32 rows (0 to 31, 32 to 63, ...) at most 9 rows name the same one
- gates_two: bfloat16 [8192, 6], P(('grp', 'ep')), may hold values from 0.049804688 to 0.3984375
- old_table: int32 [32], replicated, may hold values from 0 to 31, each once
- new_table: int32 [32], replicated, may hold values from 0 to 31, each once
- gate_up: bfloat16 [32, 2048, 1408], P('ep'), may hold values from -0.125 to 0.125
- down_proj: bfloat16 [32, 704, 2048], P('ep'), may hold values from -0.21875 to 0.21875
- norm_gain: bfloat16 [2048], replicated, may hold values from 0.099609375 to 1.8984375
- kv_weight: bfloat16 [2048, 1024], P(None, 'grp'), may hold values from -0.125 to 0.125
Outputs:
- hidden_one: bfloat16 [8192, 2048], P(('grp', 'ep'))
- kv_one: bfloat16 [8192, 1024], P(('grp', 'ep'))
- hidden_two: bfloat16 [8192, 2048], P(('grp', 'ep'))
- kv_two: bfloat16 [8192, 1024], P(('grp', 'ep'))
- gate_up_new: bfloat16 [32, 2048, 1408], P('ep', 'grp')
- down_proj_new: bfloat16 [32, 704, 2048], P('ep', None, 'grp')
The draws below stay inside these ranges and needn't reach their ends.
Inputs may be any that keep to these rules, and one draw needn't show every extreme that they name: `routes_one`: each row names 6 different slots; among the rows of one device no slot is named by more than 9 routes, a bound that some block reaches. `routes_two`: each row names 6 different slots; among the rows of one device no slot is named by more than 9 routes, a bound that some block reaches. `old_table`: each expert appears once. `new_table`: each expert appears once.
All inputs are finite; a program needn't handle non-finite values.
Results may differ from the reference program's by a relative error of at most 0.006.
Values may be sent and summed in bfloat16 or wider, within the bound.
A program may use at most 128 MiB of HBM per device.

```python
import math
import jax
import jax.numpy as jnp
import numpy as np
from jax import lax

D = 2048
FFE = 704
TOP = 6
TOK_DEV = 32
EXPERTS = 32
CAP = 9
KVW = 1024
TOKENS = 8192
N_GRP = 8
N_EP = 32


def block_scale(stream_key, extent, shards, smallest, top_value):
    def one(dim, blocks):
        steps = jax.random.uniform(jax.random.fold_in(jax.random.fold_in(stream_key, 6), dim), (blocks,), jnp.float32, smallest / len(shards), top_value / len(shards))
        return jnp.repeat(jnp.exp(steps), extent[dim] // blocks).reshape((-1,) + (1,) * (len(extent) - dim - 1))

    gain = one(*shards[0])
    for cut in shards[1:]:
        gain = gain * one(*cut)
    return gain


def shared_out(own_key, own, number, rows, count, top, most, lean):
    order = jax.random.permutation(own_key, count)
    packed, ordinary = portions_of(count, rows * top, most, lean, True), portions_of(count, rows * top, most, lean, False)
    places = jnp.arange(count)

    def named(sizes, offset_by):
        used = int((sizes > 0).sum())
        fixed = max(1, used // 4)
        shifted = fixed + (places - fixed + offset_by * (used - fixed)) % max(1, count - fixed)
        return jnp.zeros((count,), jnp.int32).at[order[jnp.where(places < fixed, places, shifted)]].set(jnp.asarray(sizes, jnp.int32))

    sizes = jnp.where(number % 4 == 0, named(packed, number // 4), named(ordinary, number - number // 4 - 1))
    mixed = jax.random.permutation(jax.random.fold_in(own, 3), count)
    donor, taker = mixed[0:count // 2 * 2:2], mixed[1:count // 2 * 2:2]
    room = jnp.minimum(sizes[donor] - 1, most - sizes[taker]) // 2
    room = jnp.where((donor == order[0]) | (taker == order[0]) | (sizes[taker] == 0), 0, jnp.maximum(room, 0))
    shifted = jax.random.randint(jax.random.fold_in(own, 4), (count // 2,), 0, 1 << 20) % (room + 1)
    sizes = sizes.at[donor].add(-shifted).at[taker].add(shifted)
    members = jnp.searchsorted(jnp.cumsum(sizes), jnp.arange(rows * top), side="right").astype(jnp.int32)
    grid = members.reshape(top, rows).T
    grid = grid[jax.random.permutation(jax.random.fold_in(own, 1), rows)]
    offset_by = jax.random.randint(jax.random.fold_in(own, 2), (rows, 1), 0, top)
    return jnp.take_along_axis(grid, (jnp.arange(top)[None, :] + offset_by) % top, axis=1)


def portions_of(amount, total, reach, slope, full):
    portions = [(1 << 20) // math.isqrt(rank ** slope) + 1 for rank in range(1, amount + 1)]
    largest = reach if full else min(reach, max(-(-total // amount), total * portions[0] // sum(portions)))
    least = 1 if total - largest >= amount - 1 else 0
    holding, surplus = [largest] + [least] * (amount - 1), total - largest - least * (amount - 1)
    while surplus > 0:
        candidates = [i for i in range(1, amount) if holding[i] < largest] or [i for i in range(1, amount) if holding[i] < reach]
        mass, budget = sum([portions[i] for i in candidates]), surplus
        for i in candidates:
            addition = min(reach - holding[i], max(1, budget * portions[i] // mass), surplus)
            holding[i] = holding[i] + addition
            surplus = surplus - addition
    return np.array(holding)


def normal_values(own_key, dims, width, most, shards=(), kind=jnp.bfloat16):
    loudness = block_scale(own_key, dims, shards, -0.22, 0.18) if shards else 1.0
    values = jax.random.normal(own_key, dims, jnp.float32) * width * loudness
    return jnp.minimum(jnp.maximum(values, -most), most).astype(kind)


def setup_inputs(seed: int = 0) -> dict:
    seeds = jax.random.split(jax.random.key(seed), 13)
    tokens_one = normal_values(seeds[0], (TOKENS, D), 1.0, 6.0, ((0, 256),))
    routes_one_keys = jax.random.split(jax.random.fold_in(seeds[1], 1), TOKENS // TOK_DEV)
    routes_one_turns = jax.random.permutation(jax.random.fold_in(seeds[1], 3), TOKENS // TOK_DEV)
    routes_one = jax.vmap(lambda own, number: shared_out(jax.random.fold_in(seeds[1], 2), own, number, TOK_DEV, EXPERTS, TOP, CAP, 2))(routes_one_keys, routes_one_turns).reshape((TOKENS, TOP))
    gates_one = jnp.clip(0.049804688 + 0.3486328 * jax.random.uniform(seeds[2], (TOKENS, TOP), jnp.float32) ** block_scale(seeds[2], (TOKENS, TOP), ((0, 256),), -0.2, 0.2), 0.049804688, 0.3984375).astype(jnp.bfloat16)
    tokens_two = normal_values(seeds[3], (TOKENS, D), 1.0, 6.0, ((0, 256),))
    routes_two_keys = jax.random.split(jax.random.fold_in(seeds[4], 1), TOKENS // TOK_DEV)
    routes_two_turns = jax.random.permutation(jax.random.fold_in(seeds[4], 3), TOKENS // TOK_DEV)
    routes_two = jax.vmap(lambda own, number: shared_out(jax.random.fold_in(seeds[4], 2), own, number, TOK_DEV, EXPERTS, TOP, CAP, 2))(routes_two_keys, routes_two_turns).reshape((TOKENS, TOP))
    gates_two = jnp.clip(0.049804688 + 0.3486328 * jax.random.uniform(seeds[5], (TOKENS, TOP), jnp.float32) ** block_scale(seeds[5], (TOKENS, TOP), ((0, 256),), -0.2, 0.2), 0.049804688, 0.3984375).astype(jnp.bfloat16)
    old_table = jax.random.permutation(seeds[6], EXPERTS).astype(jnp.int32)
    new_table = jax.random.permutation(seeds[7], EXPERTS).astype(jnp.int32)
    gate_up = normal_values(seeds[8], (EXPERTS, D, 2 * FFE), D ** -0.5, 0.125, ((0, 32),))
    down_proj = normal_values(seeds[9], (EXPERTS, FFE, D), FFE ** -0.5, 0.21875, ((0, 32),))
    norm_gain = jnp.clip(1.0 + 0.18 * jax.random.normal(seeds[10], (D,), jnp.float32), 0.099609375, 1.8984375).astype(jnp.bfloat16)
    kv_weight = normal_values(seeds[11], (D, KVW), D ** -0.5, 0.125, ((1, 8),))
    return dict(tokens_one=tokens_one, routes_one=routes_one, gates_one=gates_one, tokens_two=tokens_two, routes_two=routes_two, gates_two=gates_two, old_table=old_table, new_table=new_table, gate_up=gate_up, down_proj=down_proj, norm_gain=norm_gain, kv_weight=kv_weight)


def expert_ffn(activation, weight_in, weight_out):
    joined = jnp.dot(activation, weight_in, preferred_element_type=jnp.float32)
    gate_part = joined[:, :FFE]
    upward = joined[:, FFE:]
    hidden = (jax.nn.silu(gate_part) * upward).astype(jnp.bfloat16)
    return jnp.dot(hidden, weight_out, preferred_element_type=jnp.float32).astype(jnp.bfloat16)

def routed_layer(tokens, owners, gate_share, gate_up, down_proj):
    flattened = owners.reshape(-1).astype(jnp.int32)
    entries = flattened.shape[0]
    ordering = jnp.argsort(flattened, stable=True).astype(jnp.int32)
    numbers = jnp.arange(EXPERTS, dtype=jnp.int32)
    counts = lax.optimization_barrier(jnp.sum((flattened[:, None] == numbers[None, :]).astype(jnp.int32), axis=0))
    starts = (jnp.cumsum(counts) - counts).astype(jnp.int32)
    longest = N_GRP * N_EP * CAP
    padded = jnp.concatenate([ordering, jnp.full((longest,), entries, jnp.int32)])

    def visit_one(collected, expert):
        chosen = lax.dynamic_slice(padded, (starts[expert],), (longest,))
        chosen = jnp.where(jnp.arange(longest, dtype=jnp.int32) < counts[expert], chosen, entries)
        activation = tokens[jnp.minimum(chosen, entries - 1) // TOP]
        result = expert_ffn(activation, gate_up[expert], down_proj[expert])
        return (collected.at[chosen].set(result), None)
    collected = lax.scan(visit_one, jnp.zeros((entries + 1, D), jnp.bfloat16), numbers)[0]
    outputs = collected[:entries].reshape(tokens.shape[0], TOP, D).astype(jnp.float32)
    mixture = jnp.einsum('tk,tkd->td', gate_share.astype(jnp.float32), outputs)
    return (tokens.astype(jnp.float32) + mixture).astype(jnp.bfloat16)

def rms_norm(hidden, norm_gain):
    values = hidden.astype(jnp.float32)
    inverse_rms = lax.rsqrt(lax.optimization_barrier(jnp.mean(values * values, axis=-1, keepdims=True)) + 1e-06)
    return (values * inverse_rms * norm_gain.astype(jnp.float32)).astype(jnp.bfloat16)

def reference(tokens_one, routes_one, gates_one, tokens_two, routes_two, gates_two, old_table, new_table, gate_up, down_proj, norm_gain, kv_weight):
    old_inverse = jnp.zeros((EXPERTS,), jnp.int32).at[old_table].set(jnp.arange(EXPERTS, dtype=jnp.int32))
    sources_new = old_inverse[new_table].astype(jnp.int32)
    gate_up_new = gate_up[sources_new]
    down_proj_new = down_proj[sources_new]
    hidden_one = routed_layer(tokens_one, routes_one, gates_one, gate_up, down_proj)
    hidden_two = routed_layer(tokens_two, routes_two, gates_two, gate_up_new, down_proj_new)
    kv_one = jnp.dot(rms_norm(hidden_one, norm_gain), kv_weight, preferred_element_type=jnp.float32).astype(jnp.bfloat16)
    kv_two = jnp.dot(rms_norm(hidden_two, norm_gain), kv_weight, preferred_element_type=jnp.float32).astype(jnp.bfloat16)
    return (hidden_one, kv_one, hidden_two, kv_two, gate_up_new, down_proj_new)
```

```python
import jax
import jax.numpy as jnp
from jax import lax
from jax.sharding import PartitionSpec as P

TOP = 6


def slot_table(owners, ep_size, offset):
    rows = owners.shape[0]
    hits = (owners[:, :, None] == jnp.arange(ep_size, dtype=jnp.int32)[None, None, :])
    named = jnp.any(hits, axis=1)
    lower = jnp.tril(jnp.ones((rows, rows), jnp.float32), -1)
    rank = jnp.dot(lower, named.astype(jnp.float32), preferred_element_type=jnp.float32)
    return jnp.where(named, rank.astype(jnp.int32) + offset, -1), hits


def gate_table(hits, gates):
    return jnp.sum(jnp.where(hits, gates.astype(jnp.float32)[:, :, None], 0.0), axis=1)


def local(
    tokens_one,
    routes_one,
    gates_one,
    tokens_two,
    routes_two,
    gates_two,
    old_table,
    new_table,
    gate_up,
    down_proj,
    norm_gain,
    kv_weight,
):
    weight_in = gate_up[0]
    weight_out = down_proj[0]
    ep_size = lax.axis_size("ep")
    grp_size = lax.axis_size("grp")
    numbers = jnp.arange(ep_size, dtype=jnp.int32)
    old_inverse = jnp.sum((old_table[:, None] == numbers[None, :]).astype(jnp.int32) * numbers[:, None], axis=0)
    wanted = (new_table[:, None] == numbers[None, :]).astype(jnp.int32)
    sources_new = jnp.sum(wanted * old_inverse[None, :], axis=1)
    features, inner = weight_in.shape[0], weight_out.shape[0]
    part = features // grp_size
    start = lax.axis_index("grp") * part
    piece_in = lax.dynamic_slice_in_dim(weight_in, start, part, 0)
    piece_out = lax.dynamic_slice_in_dim(weight_out, start, part, 1)
    n_in, n_out = piece_in.size // ep_size, piece_out.size // ep_size
    pieces = jnp.concatenate(
        [piece_in.reshape(ep_size, n_in // 128, 128), piece_out.reshape(ep_size, n_out // 128, 128)], axis=1
    )
    spread = lax.all_to_all(pieces, "ep", split_axis=0, concat_axis=0, tiled=True)

    rows = tokens_one.shape[0]
    capacity = 3 * rows * TOP // (2 * ep_size)
    owners_two = jnp.sum(
        (routes_two[:, :, None] == numbers[None, None, :]).astype(jnp.int32) * sources_new[None, None, :], axis=2
    )
    table_one, hits_one = slot_table(routes_one, ep_size, 0)
    table_two, hits_two = slot_table(owners_two, ep_size, capacity)
    table = jnp.concatenate([table_one, table_two], axis=0)
    gates = jnp.concatenate([gate_table(hits_one, gates_one), gate_table(hits_two, gates_two)], axis=0)
    tokens = jnp.concatenate([tokens_one, tokens_two], axis=0)
    both = 2 * rows
    slots = jnp.arange(2 * capacity, dtype=jnp.int32)
    chosen = table[:, :, None] == slots[None, None, :]
    pick = chosen.astype(jnp.bfloat16).reshape(both, ep_size * 2 * capacity)
    mix = jnp.where(chosen, gates[:, :, None], 0.0).astype(jnp.bfloat16).reshape(both, ep_size * 2 * capacity)
    packed = lax.dot_general(
        pick, tokens, (((0,), (0,)), ((), ())), preferred_element_type=jnp.float32
    ).astype(jnp.bfloat16)
    arrived = lax.all_to_all(
        packed.reshape(ep_size, 2 * capacity, features), "ep", split_axis=0, concat_axis=0, tiled=True
    )
    activation = arrived.reshape(ep_size * 2 * capacity, features)
    joined = jnp.dot(activation, weight_in, preferred_element_type=jnp.float32)
    hidden = (jax.nn.silu(joined[:, :inner]) * joined[:, inner:]).astype(jnp.bfloat16)
    result = jnp.dot(hidden, weight_out, preferred_element_type=jnp.float32).astype(jnp.bfloat16)
    returned = lax.all_to_all(
        result.reshape(ep_size, 2 * capacity, features), "ep", split_axis=0, concat_axis=0, tiled=True
    ).reshape(ep_size * 2 * capacity, features)
    collected = lax.all_to_all(spread[sources_new], "ep", split_axis=0, concat_axis=0, tiled=True)
    cut = n_in // 128
    gate_up_new = collected[:, :cut].reshape(1, part, 2 * inner)
    down_proj_new = collected[:, cut:].reshape(1, inner, part)
    mixture = jnp.dot(mix, returned, preferred_element_type=jnp.float32)
    out = (tokens.astype(jnp.float32) + mixture).astype(jnp.bfloat16)
    values = out.astype(jnp.float32)
    inverse_rms = lax.rsqrt(jnp.mean(values * values, axis=-1, keepdims=True) + 1e-06)
    normed = (values * inverse_rms * norm_gain.astype(jnp.float32)).astype(jnp.bfloat16)
    projected = jnp.dot(
        normed,
        lax.all_gather(kv_weight, "grp", axis=1, tiled=True),
        preferred_element_type=jnp.float32,
    ).astype(jnp.bfloat16)
    return (out[:rows], projected[:rows], out[rows:], projected[rows:], gate_up_new, down_proj_new)


def solution(mesh):
    split = P(("grp", "ep"), None)
    return jax.shard_map(
        local,
        mesh=mesh,
        in_specs=(split,) * 6 + (P(), P(), P("ep", None, None), P("ep", None, None), P(), P(None, "grp")),
        out_specs=(split,) * 4 + (P("ep", "grp", None), P("ep", None, "grp")),
        check_vma=False,
    )
```

```python
import jax
import jax.numpy as jnp
from jax import lax
from jax.experimental import pallas as pl
from jax.experimental.pallas import tpu as pltpu
from jax.sharding import PartitionSpec as P

TOP = 6
CHUNKS = 4
BF, F32 = jnp.bfloat16, jnp.float32
MESH = pl.DeviceIdType.MESH


def above(values, step, count):
    total = jnp.zeros_like(values)
    for i in range(1, count):
        total = total + (values >= i * step).astype(jnp.int32)
    return total


def iota(shape, dim):
    return lax.broadcasted_iota(jnp.int32, shape, dim)


def token_kernel(
    t1_ref, r1_ref, g1_ref, t2_ref, r2_ref, g2_ref, old_ref, new_ref, win_hbm, wout_hbm, o_ref,
    win, wout, tab, tabs, zbuf, pbuf, abuf, joined, rbuf, cbuf, sbuf, gbuf, own,
    wsem, tsend, trecv, zsend, zrecv, ysend, yrecv, rsend, rrecv, bsend, brecv,
):
    rows = t1_ref.shape[0]
    both = 2 * rows
    width = zbuf.shape[3]
    slab = pbuf.shape[2]
    cap = slab // 8
    inner = wout.shape[0]
    grp, ep = lax.axis_index("grp"), lax.axis_index("ep")
    x, low = grp % 4, grp // 4
    y, high, core = ep // 8, (ep // 2) % 4, ep % 2
    z = high * 2 + low
    sign = 1 - 2 * low
    me = y * 2 + core

    def at_z(step):
        there = (z + 8 + step) % 8
        return ((there % 2) * 4 + x, (y * 4 + there // 2) * 2 + core)

    def at_q(q):
        return (grp, ((q // 2) * 4 + high) * 2 + q % 2)

    z_to = (2 * sign, -3 * sign, -sign)
    z_from = (-2 * sign, -3 * sign, -sign)

    win_copy = pltpu.make_async_copy(win_hbm.at[0], win, wsem.at[0])
    wout_copy = pltpu.make_async_copy(wout_hbm.at[0], wout, wsem.at[1])
    win_copy.start()
    wout_copy.start()

    barrier = pltpu.get_barrier_semaphore()
    for step in (2, -2, -3 * sign, -sign):
        pl.semaphore_signal(barrier, inc=1, device_id=at_z(step), device_id_type=MESH)
    for off in range(1, 8):
        pl.semaphore_signal(barrier, inc=1, device_id=at_q((me + off) % 8), device_id_type=MESH)

    lane = iota((rows, 128), 1)

    def named_and_gates(r_ref, g_ref):
        named = jnp.zeros((rows, 128), F32)
        gate = jnp.zeros((rows, 128), F32)
        for k in range(TOP):
            hit = r_ref[:, k:k + 1] == lane
            named = named + jnp.where(hit, 1.0, 0.0)
            gate = gate + jnp.where(hit, g_ref[:, k:k + 1].astype(F32), 0.0)
        return named, gate

    same = (new_ref[...] == old_ref[...]).astype(F32).astype(BF)
    n1, gate1 = named_and_gates(r1_ref, g1_ref)
    n2, gate2 = named_and_gates(r2_ref, g2_ref)
    n2 = jnp.dot(n2[:, :32].astype(BF), same, preferred_element_type=F32)
    gate2 = jnp.dot(gate2[:, :32].astype(BF), same, preferred_element_type=F32)
    earlier = (iota((rows, rows), 1) < iota((rows, rows), 0)).astype(F32).astype(BF)

    def entries(named, gate, offset):
        rank = jnp.dot(earlier, named.astype(BF), preferred_element_type=F32)
        return jnp.where(named > 0.5, rank + offset, -1.0), pltpu.roll(gate, 32, 1)

    v1, w1 = entries(n1, gate1, 0.0)
    v2, w2 = entries(n2, gate2, float(cap))
    tab[:rows] = jnp.where(lane < 32, v1, w1).astype(BF)
    tab[rows:] = jnp.where(lane < 32, v2, w2).astype(BF)
    tabs[0] = tab[...]

    def place(k, carry):
        columns = pl.ds(pl.multiple_of(k * width, width), width)
        zbuf[k, 0, :rows] = t1_ref[:, columns]
        zbuf[k, 0, rows:] = t2_ref[:, columns]
        return carry

    lax.fori_loop(0, CHUNKS, place, 0)
    pl.semaphore_wait(barrier, 11)

    def tab_copy(m):
        return pltpu.make_async_remote_copy(
            src_ref=tab, dst_ref=tabs.at[m + 1], send_sem=tsend.at[m], recv_sem=trecv.at[m],
            device_id=at_z(z_to[m]), device_id_type=MESH)

    def z_copy(k, m):
        return pltpu.make_async_remote_copy(
            src_ref=zbuf.at[k, 0], dst_ref=zbuf.at[k, m + 1], send_sem=zsend.at[k, m], recv_sem=zrecv.at[k, m],
            device_id=at_z(z_to[m]), device_id_type=MESH)

    def y_copy(k, off):
        q = (me + off) % 8
        return pltpu.make_async_remote_copy(
            src_ref=pbuf.at[k, q], dst_ref=abuf.at[k, me], send_sem=ysend.at[k, off], recv_sem=yrecv.at[k, off],
            device_id=at_q(q), device_id_type=MESH)

    def r_copy(k, off):
        q = (me + 8 - off) % 8
        return pltpu.make_async_remote_copy(
            src_ref=rbuf.at[k, q], dst_ref=cbuf.at[k, me], send_sem=rsend.at[k, off], recv_sem=rrecv.at[k, off],
            device_id=at_q(q), device_id_type=MESH)

    def b_copy(k, m):
        return pltpu.make_async_remote_copy(
            src_ref=sbuf.at[k, m], dst_ref=gbuf.at[k, m], send_sem=bsend.at[k, m], recv_sem=brecv.at[k, m],
            device_id=at_z(z_from[m]), device_id_type=MESH)

    for m in range(3):
        tab_copy(m).start()

    def send_z(k, carry):
        for m in range(3):
            z_copy(k, m).start()
        return carry

    lax.fori_loop(0, CHUNKS, send_z, 0)
    for m in range(3):
        tab_copy(m).wait_recv()

    total = 8 * slab
    gathered = 4 * both
    table = tabs[...].reshape(gathered, 128)

    def expert_of(q):
        return (q // 2) * 8 + high * 2 + q % 2

    def slot_facts(shape, dim):
        n = iota(shape, dim)
        q = above(n, slab, 8)
        inside = n - q * slab
        j = above(inside, 2 * cap, 4)
        half = above(q, 2, 4)
        return half * 8 + high * 2 + (q - 2 * half), j, (inside - j * 2 * cap).astype(F32)

    e_row, _, _ = slot_facts((total, 128), 0)
    choose = (iota((total, 128), 1) == e_row).astype(F32).astype(BF)
    found = lax.dot_general(choose, table, (((1,), (1,)), ((), ())), preferred_element_type=F32)
    _, j_row, r_row = slot_facts((total, gathered), 0)
    pick = ((found == r_row) & (j_row == above(iota((total, gathered), 1), both, 4))).astype(F32).astype(BF)
    e_col, _, _ = slot_facts((128, total), 1)
    choose_v = (iota((128, total), 0) == e_col).astype(F32).astype(BF)
    choose_g = (iota((128, total), 0) == e_col + 32).astype(F32).astype(BF)
    found_v = jnp.dot(table, choose_v, preferred_element_type=F32)
    found_g = jnp.dot(table, choose_g, preferred_element_type=F32)
    _, j_col, r_col = slot_facts((gathered, total), 1)
    mix = jnp.where(
        (found_v == r_col) & (j_col == above(iota((gathered, total), 0), both, 4)), found_g, 0.0).astype(BF)

    def pack(k, carry):
        for m in range(3):
            z_copy(k, m).wait_recv()
        packed = jnp.dot(pick, zbuf[k].reshape(gathered, width), preferred_element_type=F32)
        pbuf[k] = packed.reshape(8, slab, width).astype(BF)
        for off in range(1, 8):
            y_copy(k, off).start()
        abuf[k, me] = pbuf[k, me]
        return carry

    lax.fori_loop(0, CHUNKS, pack, 0)
    win_copy.wait()
    joined[...] = jnp.zeros_like(joined)

    def project(k, carry):
        for off in range(1, 8):
            y_copy(k, off).wait_recv()
        block = abuf[k].reshape(total, width)
        joined[...] += jnp.dot(
            block, win[pl.ds(pl.multiple_of(k * width, width), width), :], preferred_element_type=F32)
        return carry

    lax.fori_loop(0, CHUNKS, project, 0)
    gate_part = joined[:, :inner]
    hidden = (gate_part / (1.0 + jnp.exp(-gate_part)) * joined[:, inner:]).astype(BF)
    wout_copy.wait()

    def expand(k, carry):
        result = jnp.dot(
            hidden, wout[:, pl.ds(pl.multiple_of(k * width, width), width)], preferred_element_type=F32)
        rbuf[k] = result.reshape(8, slab, width).astype(BF)
        for off in range(1, 8):
            r_copy(k, off).start()
        cbuf[k, me] = rbuf[k, me]
        return carry

    lax.fori_loop(0, CHUNKS, expand, 0)

    def combine(k, carry):
        for off in range(1, 8):
            r_copy(k, off).wait_recv()
        part = jnp.dot(mix, cbuf[k].reshape(total, width), preferred_element_type=F32)
        own[k] = part[:both]
        sbuf[k] = part[both:].reshape(3, both, width).astype(BF)
        for m in range(3):
            b_copy(k, m).start()
        return carry

    lax.fori_loop(0, CHUNKS, combine, 0)

    def finish(k, carry):
        for m in range(3):
            b_copy(k, m).wait_recv()
        sums = own[k]
        for m in range(3):
            sums = sums + gbuf[k, m].astype(F32)
        o_ref[:, pl.ds(pl.multiple_of(k * width, width), width)] = sums
        return carry

    lax.fori_loop(0, CHUNKS, finish, 0)
    for m in range(3):
        tab_copy(m).wait_send()

    def drain(k, carry):
        for m in range(3):
            z_copy(k, m).wait_send()
            b_copy(k, m).wait_send()
        for off in range(1, 8):
            y_copy(k, off).wait_send()
            r_copy(k, off).wait_send()
        return carry

    lax.fori_loop(0, CHUNKS, drain, 0)


def routed(t1, r1, g1, t2, r2, g2, old_table, new_table, gate_up, down_proj):
    rows, features = t1.shape
    both = 2 * rows
    inner = down_proj.shape[1]
    experts = old_table.shape[0]
    cap = 3 * rows * TOP // (2 * experts)
    slab = 8 * cap
    width = features // CHUNKS
    old_row = jnp.pad(old_table, (0, 128 - experts), constant_values=-1)[None, :]
    vmem = pl.BlockSpec(memory_space=pltpu.VMEM)
    hbm = pl.BlockSpec(memory_space=pl.ANY)
    dma = pltpu.SemaphoreType.DMA
    return pl.pallas_call(
        token_kernel,
        out_shape=jax.ShapeDtypeStruct((both, features), F32),
        in_specs=[vmem] * 8 + [hbm] * 2,
        out_specs=vmem,
        scratch_shapes=[
            pltpu.VMEM((features, 2 * inner), BF),
            pltpu.VMEM((inner, features), BF),
            pltpu.VMEM((both, 128), BF),
            pltpu.VMEM((4, both, 128), BF),
            pltpu.VMEM((CHUNKS, 4, both, width), BF),
            pltpu.VMEM((CHUNKS, 8, slab, width), BF),
            pltpu.VMEM((CHUNKS, 8, slab, width), BF),
            pltpu.VMEM((8 * slab, 2 * inner), F32),
            pltpu.VMEM((CHUNKS, 8, slab, width), BF),
            pltpu.VMEM((CHUNKS, 8, slab, width), BF),
            pltpu.VMEM((CHUNKS, 3, both, width), BF),
            pltpu.VMEM((CHUNKS, 3, both, width), BF),
            pltpu.VMEM((CHUNKS, both, width), F32),
            dma((2,)), dma((3,)), dma((3,)),
            dma((CHUNKS, 3)), dma((CHUNKS, 3)),
            dma((CHUNKS, 8)), dma((CHUNKS, 8)),
            dma((CHUNKS, 8)), dma((CHUNKS, 8)),
            dma((CHUNKS, 3)), dma((CHUNKS, 3)),
        ],
        compiler_params=pltpu.CompilerParams(
            collective_id=0, has_side_effects=True, vmem_limit_bytes=50 << 20),
        cost_estimate=pl.CostEstimate(flops=8_000_000_000, bytes_accessed=200_000_000, transcendentals=0),
        name="routed_tokens",
    )(t1, r1, g1, t2, r2, g2, old_row, new_table[:, None], gate_up, down_proj)


def local(
    tokens_one,
    routes_one,
    gates_one,
    tokens_two,
    routes_two,
    gates_two,
    old_table,
    new_table,
    gate_up,
    down_proj,
    norm_gain,
    kv_weight,
):
    weight_in = gate_up[0]
    weight_out = down_proj[0]
    ep_size = lax.axis_size("ep")
    grp_size = lax.axis_size("grp")
    numbers = jnp.arange(ep_size, dtype=jnp.int32)
    sources_new = jnp.sum((new_table[:, None] == old_table[None, :]).astype(jnp.int32) * numbers[None, :], axis=1)
    features, inner = weight_in.shape[0], weight_out.shape[0]
    part = features // grp_size
    start = lax.axis_index("grp") * part
    piece_in = lax.dynamic_slice_in_dim(weight_in, start, part, 0)
    piece_out = lax.dynamic_slice_in_dim(weight_out, start, part, 1)
    n_in, n_out = piece_in.size // ep_size, piece_out.size // ep_size
    pieces = jnp.concatenate(
        [piece_in.reshape(ep_size, n_in // 128, 128), piece_out.reshape(ep_size, n_out // 128, 128)], axis=1
    )
    spread = lax.all_to_all(pieces, "ep", split_axis=0, concat_axis=0, tiled=True)
    collected = lax.all_to_all(spread[sources_new], "ep", split_axis=0, concat_axis=0, tiled=True)
    cut = n_in // 128
    gate_up_new = collected[:, :cut].reshape(1, part, 2 * inner)
    down_proj_new = collected[:, cut:].reshape(1, inner, part)

    rows = tokens_one.shape[0]
    mixture = routed(
        tokens_one, routes_one, gates_one, tokens_two, routes_two, gates_two, old_table, new_table,
        gate_up, down_proj)
    tokens = jnp.concatenate([tokens_one, tokens_two], axis=0)
    out = (tokens.astype(F32) + mixture).astype(BF)
    values = out.astype(F32)
    inverse_rms = lax.rsqrt(jnp.mean(values * values, axis=-1, keepdims=True) + 1e-06)
    normed = (values * inverse_rms * norm_gain.astype(F32)).astype(BF)
    projected = jnp.dot(
        normed,
        lax.all_gather(kv_weight, "grp", axis=1, tiled=True),
        preferred_element_type=F32,
    ).astype(BF)
    return (out[:rows], projected[:rows], out[rows:], projected[rows:], gate_up_new, down_proj_new)


def solution(mesh):
    split = P(("grp", "ep"), None)
    return jax.shard_map(
        local,
        mesh=mesh,
        in_specs=(split,) * 6 + (P(), P(), P("ep", None, None), P("ep", None, None), P(), P(None, "grp")),
        out_specs=(split,) * 4 + (P("ep", "grp", None), P("ep", None, "grp")),
        check_vma=False,
    )
```

```python
import jax
import jax.numpy as jnp
from jax import lax
from jax.experimental import pallas as pl
from jax.experimental.pallas import tpu as pltpu
from jax.sharding import PartitionSpec as P

TOP = 6
CHUNKS = 4
BF, F32 = jnp.bfloat16, jnp.float32
MESH = pl.DeviceIdType.MESH


def above(values, step, count):
    total = jnp.zeros_like(values)
    for i in range(1, count):
        total = total + (values >= i * step).astype(jnp.int32)
    return total


def iota(shape, dim):
    return lax.broadcasted_iota(jnp.int32, shape, dim)


def token_kernel(
    t1_ref, r1_ref, g1_ref, t2_ref, r2_ref, g2_ref, old_ref, new_ref, win_hbm, wout_hbm,
    o_ref, in_new, out_new,
    r1v, g1v, r2v, g2v, oldv, newv, srcv, srcs, mid_in, mid_out, pick_in, pick_out, fin_out,
    win, wout, ttab, tab, tabs, zbuf, pbuf, abuf, joined, rbuf, cbuf, sbuf, gbuf, own,
    wsem, lsem, tsend, trecv, zsend, zrecv, ysend, yrecv, rsend, rrecv, bsend, brecv,
    hsend, hrecv, fsend, frecv, selfsem,
):
    rows = t1_ref.shape[0]
    both = 2 * rows
    width = zbuf.shape[3]
    slab = pbuf.shape[2]
    cap = slab // 8
    inner = wout.shape[0]
    grp, ep = lax.axis_index("grp"), lax.axis_index("ep")
    x, low = grp % 4, grp // 4
    y, high, core = ep // 8, (ep // 2) % 4, ep % 2
    z = high * 2 + low
    sign = 1 - 2 * low
    me = y * 2 + core

    def at_z(step):
        there = (z + 8 + step) % 8
        return ((there % 2) * 4 + x, (y * 4 + there // 2) * 2 + core)

    def at_q(q):
        return (grp, ((q // 2) * 4 + high) * 2 + q % 2)

    z_to = (2 * sign, -3 * sign, -sign)
    z_from = (-2 * sign, -3 * sign, -sign)

    copies = [
        pltpu.make_async_copy(r1_ref, r1v, lsem.at[0]),
        pltpu.make_async_copy(g1_ref, g1v, lsem.at[1]),
        pltpu.make_async_copy(r2_ref, r2v, lsem.at[2]),
        pltpu.make_async_copy(g2_ref, g2v, lsem.at[3]),
        pltpu.make_async_copy(old_ref, oldv, lsem.at[7]),
        pltpu.make_async_copy(new_ref, newv, lsem.at[8]),
    ]
    for copy in copies:
        copy.start()

    def place_copy(k, b):
        t_ref = t1_ref if b == 0 else t2_ref
        return pltpu.make_async_copy(
            t_ref.at[:, pl.ds(pl.multiple_of(k * width, width), width)], zbuf.at[k, 0, pl.ds(b * rows, rows)],
            lsem.at[4 + b])

    for k in range(CHUNKS):
        for b in range(2):
            place_copy(k, b).start()
    win_copy = pltpu.make_async_copy(win_hbm.at[0], win, wsem.at[0])
    wout_copy = pltpu.make_async_copy(wout_hbm.at[0], wout, wsem.at[1])
    win_copy.start()
    wout_copy.start()

    def at_ep(e):
        return (grp, e)

    barrier = pltpu.get_barrier_semaphore()
    for step in (2, -2, -3 * sign, -sign):
        pl.semaphore_signal(barrier, inc=1, device_id=at_z(step), device_id_type=MESH)

    def greet(off, carry):
        pl.semaphore_signal(barrier, inc=1, device_id=at_ep((ep + off) % 32), device_id_type=MESH)
        return carry

    lax.fori_loop(1, 32, greet, 0)

    for copy in copies:
        copy.wait()
    square = (32, 32)

    def named_and_gates(r_ref, g_ref):
        named = jnp.zeros((32, rows), F32)
        gate = jnp.zeros((32, rows), F32)
        number = iota((32, rows), 0)
        for k in range(TOP):
            hit = r_ref[k:k + 1, :] == number
            named = named + jnp.where(hit, 1.0, 0.0)
            gate = gate + jnp.where(hit, g_ref[k:k + 1, :].astype(F32), 0.0)
        return named, gate

    diagonal = iota(square, 0) == iota(square, 1)
    old_column = jnp.sum(jnp.where(diagonal, oldv[...].astype(F32), 0.0), axis=1, keepdims=True)
    same = (old_column == newv[...].astype(F32)).astype(F32)
    found_at = jnp.sum(same * iota(square, 0).astype(F32), axis=0, keepdims=True)
    srcv[:, :32] = found_at.astype(jnp.int32)
    src_copy = pltpu.make_async_copy(srcv, srcs, lsem.at[6])
    src_copy.start()
    same = same.astype(BF)
    n1, gate1 = named_and_gates(r1v, g1v)
    n2, gate2 = named_and_gates(r2v, g2v)
    n2 = jnp.dot(same, n2.astype(BF), preferred_element_type=F32)
    gate2 = jnp.dot(same, gate2.astype(BF), preferred_element_type=F32)
    earlier = (iota((rows, rows), 0) < iota((rows, rows), 1)).astype(F32).astype(BF)

    def entries(named, offset):
        rank = jnp.dot(named.astype(BF), earlier, preferred_element_type=F32)
        return jnp.where(named > 0.5, rank + offset, -1.0)

    ttab[...] = jnp.zeros_like(ttab)
    ttab[:32, :rows] = entries(n1, 0.0)
    ttab[:32, rows:both] = entries(n2, float(cap))
    ttab[32:64, :rows] = gate1
    ttab[32:64, rows:both] = gate2
    tab[...] = jnp.transpose(ttab[...])[:both].astype(BF)
    tabs[0] = tab[...]
    for b in range(2):
        for k in range(CHUNKS):
            place_copy(k, b).wait()
    pl.semaphore_wait(barrier, 35)

    def part_in(j):
        return win_hbm.at[0, pl.ds(pl.multiple_of(grp * 256 + j * 8, 8), 8), :]

    def part_out(j):
        p = j // 2
        return wout_hbm.at[
            0, pl.ds(pl.multiple_of(8 * ((11 * p) // 2), 8), 48),
            pl.ds(pl.multiple_of(grp * 256 + (j % 2) * 128, 128), 128)]

    def ep_of(dy, dz, dc):
        return (((y + dy) % 4) * 4 + (high + dz) % 4) * 2 + (core + dc) % 2

    def ep_at(n, back):
        dy, dz, dc = (n // 2) % 4, n // 8, n % 2
        if back:
            return ep_of(4 - dy, 4 - dz, dc)
        return ep_of(dy, dz, dc)

    def spread_copies(n):
        j = ep_at(n, False)
        return [
            pltpu.make_async_remote_copy(
                src_ref=part_in(j), dst_ref=mid_in.at[ep], send_sem=hsend.at[0, n], recv_sem=hrecv.at[0, n],
                device_id=at_ep(j), device_id_type=MESH),
            pltpu.make_async_remote_copy(
                src_ref=part_out(j), dst_ref=mid_out.at[ep], send_sem=hsend.at[1, n], recv_sem=hrecv.at[1, n],
                device_id=at_ep(j), device_id_type=MESH)]

    def fetch_copies(n):
        s = ep_at(n, False)
        return [
            pltpu.make_async_remote_copy(
                src_ref=pick_in.at[s], dst_ref=in_new.at[pl.ds(pl.multiple_of(ep * 8, 8), 8), :],
                send_sem=fsend.at[0, n], recv_sem=frecv.at[0, n],
                device_id=at_ep(s), device_id_type=MESH),
            pltpu.make_async_remote_copy(
                src_ref=pick_out.at[s], dst_ref=fin_out.at[ep], send_sem=fsend.at[1, n], recv_sem=frecv.at[1, n],
                device_id=at_ep(s), device_id_type=MESH)]

    def start_spread(n, carry):
        for copy in spread_copies(n):
            copy.start()
        return carry

    def wait_spread(n, carry):
        for copy in spread_copies(n):
            copy.wait_recv()
        return carry

    own_spread = [
        pltpu.make_async_copy(part_in(ep), mid_in.at[ep], selfsem.at[0]),
        pltpu.make_async_copy(part_out(ep), mid_out.at[ep], selfsem.at[1])]
    own_fetch = [
        pltpu.make_async_copy(pick_in.at[ep], in_new.at[pl.ds(pl.multiple_of(ep * 8, 8), 8), :], selfsem.at[2]),
        pltpu.make_async_copy(pick_out.at[ep], fin_out.at[ep], selfsem.at[3])]

    def tab_copy(m):
        return pltpu.make_async_remote_copy(
            src_ref=tab, dst_ref=tabs.at[m + 1], send_sem=tsend.at[m], recv_sem=trecv.at[m],
            device_id=at_z(z_to[m]), device_id_type=MESH)

    def z_copy(k, m):
        return pltpu.make_async_remote_copy(
            src_ref=zbuf.at[k, 0], dst_ref=zbuf.at[k, m + 1], send_sem=zsend.at[k, m], recv_sem=zrecv.at[k, m],
            device_id=at_z(z_to[m]), device_id_type=MESH)

    def y_copy(k, off):
        q = (me + off) % 8
        return pltpu.make_async_remote_copy(
            src_ref=pbuf.at[k, q], dst_ref=abuf.at[k, me], send_sem=ysend.at[k, off], recv_sem=yrecv.at[k, off],
            device_id=at_q(q), device_id_type=MESH)

    def r_copy(k, off):
        q = (me + 8 - off) % 8
        return pltpu.make_async_remote_copy(
            src_ref=rbuf.at[k, q], dst_ref=cbuf.at[k, me], send_sem=rsend.at[k, off], recv_sem=rrecv.at[k, off],
            device_id=at_q(q), device_id_type=MESH)

    def b_copy(k, m):
        return pltpu.make_async_remote_copy(
            src_ref=sbuf.at[k, m], dst_ref=gbuf.at[k, m], send_sem=bsend.at[k, m], recv_sem=brecv.at[k, m],
            device_id=at_z(z_from[m]), device_id_type=MESH)

    for m in range(3):
        tab_copy(m).start()

    def send_z(k, carry):
        for m in range(3):
            z_copy(k, m).start()
        return carry

    lax.fori_loop(0, CHUNKS, send_z, 0)
    for copy in own_spread:
        copy.start()
    lax.fori_loop(1, 8, start_spread, 0)
    for m in range(3):
        tab_copy(m).wait_recv()

    total = 8 * slab
    gathered = 4 * both
    table = tabs[...].reshape(gathered, 128)

    def expert_of(q):
        return (q // 2) * 8 + high * 2 + q % 2

    def slot_facts(shape, dim):
        n = iota(shape, dim)
        q = above(n, slab, 8)
        inside = n - q * slab
        j = above(inside, 2 * cap, 4)
        half = above(q, 2, 4)
        return half * 8 + high * 2 + (q - 2 * half), j, (inside - j * 2 * cap).astype(F32)

    e_row, _, _ = slot_facts((total, 128), 0)
    choose = (iota((total, 128), 1) == e_row).astype(F32).astype(BF)
    found = lax.dot_general(choose, table, (((1,), (1,)), ((), ())), preferred_element_type=F32)
    _, j_row, r_row = slot_facts((total, gathered), 0)
    pick = ((found == r_row) & (j_row == above(iota((total, gathered), 1), both, 4))).astype(F32).astype(BF)
    e_col, _, _ = slot_facts((128, total), 1)
    choose_v = (iota((128, total), 0) == e_col).astype(F32).astype(BF)
    choose_g = (iota((128, total), 0) == e_col + 32).astype(F32).astype(BF)
    found_v = jnp.dot(table, choose_v, preferred_element_type=F32)
    found_g = jnp.dot(table, choose_g, preferred_element_type=F32)
    _, j_col, r_col = slot_facts((gathered, total), 1)
    mix = jnp.where(
        (found_v == r_col) & (j_col == above(iota((gathered, total), 0), both, 4)), found_g, 0.0).astype(BF)

    def pack(k, carry):
        for m in range(3):
            z_copy(k, m).wait_recv()
        packed = jnp.dot(pick, zbuf[k].reshape(gathered, width), preferred_element_type=F32)
        pbuf[k] = packed.reshape(8, slab, width).astype(BF)
        for off in range(1, 8):
            y_copy(k, off).start()
        abuf[k, me] = pbuf[k, me]
        return carry

    lax.fori_loop(0, CHUNKS, pack, 0)
    lax.fori_loop(8, 32, start_spread, 0)
    win_copy.wait()
    joined[...] = jnp.zeros_like(joined)

    def project(k, carry):
        for off in range(1, 8):
            y_copy(k, off).wait_recv()
        block = abuf[k].reshape(total, width)
        joined[...] += jnp.dot(
            block, win[pl.ds(pl.multiple_of(k * width, width), width), :], preferred_element_type=F32)
        return carry

    lax.fori_loop(0, CHUNKS, project, 0)
    gate_part = joined[:, :inner]
    hidden = (gate_part / (1.0 + jnp.exp(-gate_part)) * joined[:, inner:]).astype(BF)
    wout_copy.wait()

    def expand(k, carry):
        result = jnp.dot(
            hidden, wout[:, pl.ds(pl.multiple_of(k * width, width), width)], preferred_element_type=F32)
        rbuf[k] = result.reshape(8, slab, width).astype(BF)
        for off in range(1, 8):
            r_copy(k, off).start()
        cbuf[k, me] = rbuf[k, me]
        return carry

    lax.fori_loop(0, CHUNKS, expand, 0)

    src_copy.wait()
    for copy in own_spread:
        copy.wait()
    lax.fori_loop(1, 32, wait_spread, 0)

    def choose_parts(s, carry):
        wanted = jnp.minimum(jnp.maximum(srcs[0, s], 0), 31)
        pick_in[s] = mid_in[wanted]
        pick_out[s] = mid_out[wanted]
        return carry

    lax.fori_loop(0, 32, choose_parts, 0)

    def start_fetch(n, carry):
        for copy in fetch_copies(n):
            copy.start()
        return carry

    lax.fori_loop(1, 32, start_fetch, 0)
    for copy in own_fetch:
        copy.start()

    def combine(k, carry):
        for off in range(1, 8):
            r_copy(k, off).wait_recv()
        part = jnp.dot(mix, cbuf[k].reshape(total, width), preferred_element_type=F32)
        own[k] = part[:both]
        sbuf[k] = part[both:].reshape(3, both, width).astype(BF)
        for m in range(3):
            b_copy(k, m).start()
        return carry

    lax.fori_loop(0, CHUNKS, combine, 0)

    def finish(k, carry):
        for m in range(3):
            b_copy(k, m).wait_recv()
        sums = own[k]
        for m in range(3):
            sums = sums + gbuf[k, m].astype(F32)
        o_ref[:, pl.ds(pl.multiple_of(k * width, width), width)] = sums
        return carry

    lax.fori_loop(0, CHUNKS, finish, 0)

    def end_fetch(n, carry):
        for copy in spread_copies(n):
            copy.wait_send()
        for copy in fetch_copies(n):
            copy.wait_send()
            copy.wait_recv()
        return carry

    for copy in own_fetch:
        copy.wait()
    lax.fori_loop(1, 32, end_fetch, 0)
    for p in range(16):
        first, count = 8 * ((11 * p) // 2), 40 + 8 * (p % 2)
        for h in range(2):
            out_new[first:first + count, 128 * h:128 * h + 128] = fin_out[2 * p + h, :count]
    for m in range(3):
        tab_copy(m).wait_send()

    def drain(k, carry):
        for m in range(3):
            z_copy(k, m).wait_send()
            b_copy(k, m).wait_send()
        for off in range(1, 8):
            y_copy(k, off).wait_send()
            r_copy(k, off).wait_send()
        return carry

    lax.fori_loop(0, CHUNKS, drain, 0)


def routed(t1, r1, g1, t2, r2, g2, old_table, new_table, gate_up, down_proj):
    rows, features = t1.shape
    both = 2 * rows
    inner = down_proj.shape[1]
    experts = old_table.shape[0]
    cap = 3 * rows * TOP // (2 * experts)
    slab = 8 * cap
    width = features // CHUNKS
    vmem = pl.BlockSpec(memory_space=pltpu.VMEM)
    hbm = pl.BlockSpec(memory_space=pltpu.HBM)
    dma = pltpu.SemaphoreType.DMA
    part = features // 8
    return pl.pallas_call(
        token_kernel,
        out_shape=(
            jax.ShapeDtypeStruct((both, features), F32),
            jax.ShapeDtypeStruct((part, 2 * inner), BF),
            jax.ShapeDtypeStruct((inner, part), BF),
        ),
        in_specs=[hbm] * 10,
        out_specs=(vmem, hbm, vmem),
        scratch_shapes=[
            pltpu.VMEM((TOP, rows), jnp.int32),
            pltpu.VMEM((TOP, rows), BF),
            pltpu.VMEM((TOP, rows), jnp.int32),
            pltpu.VMEM((TOP, rows), BF),
            pltpu.VMEM((1, 32), jnp.int32),
            pltpu.VMEM((1, 32), jnp.int32),
            pltpu.VMEM((1, 128), jnp.int32),
            pltpu.SMEM((1, 128), jnp.int32),
            pltpu.VMEM((32, 8, 2 * inner), BF),
            pltpu.VMEM((32, 48, 128), BF),
            pltpu.VMEM((32, 8, 2 * inner), BF),
            pltpu.VMEM((32, 48, 128), BF),
            pltpu.VMEM((32, 48, 128), BF),
            pltpu.VMEM((features, 2 * inner), BF),
            pltpu.VMEM((inner, features), BF),
            pltpu.VMEM((128, 128), F32),
            pltpu.VMEM((both, 128), BF),
            pltpu.VMEM((4, both, 128), BF),
            pltpu.VMEM((CHUNKS, 4, both, width), BF),
            pltpu.VMEM((CHUNKS, 8, slab, width), BF),
            pltpu.VMEM((CHUNKS, 8, slab, width), BF),
            pltpu.VMEM((8 * slab, 2 * inner), F32),
            pltpu.VMEM((CHUNKS, 8, slab, width), BF),
            pltpu.VMEM((CHUNKS, 8, slab, width), BF),
            pltpu.VMEM((CHUNKS, 3, both, width), BF),
            pltpu.VMEM((CHUNKS, 3, both, width), BF),
            pltpu.VMEM((CHUNKS, both, width), F32),
            dma((2,)), dma((9,)), dma((3,)), dma((3,)),
            dma((CHUNKS, 3)), dma((CHUNKS, 3)),
            dma((CHUNKS, 8)), dma((CHUNKS, 8)),
            dma((CHUNKS, 8)), dma((CHUNKS, 8)),
            dma((CHUNKS, 3)), dma((CHUNKS, 3)),
            dma((2, 32)), dma((2, 32)), dma((2, 32)), dma((2, 32)), dma((4,)),
        ],
        compiler_params=pltpu.CompilerParams(
            collective_id=0, has_side_effects=True, vmem_limit_bytes=60 << 20),
        cost_estimate=pl.CostEstimate(flops=8_000_000_000, bytes_accessed=200_000_000, transcendentals=0),
        name="routed_tokens",
    )(t1, r1.T, g1.T, t2, r2.T, g2.T, old_table[None, :], new_table[None, :], gate_up, down_proj)


def local(
    tokens_one,
    routes_one,
    gates_one,
    tokens_two,
    routes_two,
    gates_two,
    old_table,
    new_table,
    gate_up,
    down_proj,
    norm_gain,
    kv_weight,
):
    rows = tokens_one.shape[0]
    mixture, in_new, out_new = routed(
        tokens_one, routes_one, gates_one, tokens_two, routes_two, gates_two, old_table, new_table,
        gate_up, down_proj)
    tokens = jnp.concatenate([tokens_one, tokens_two], axis=0)
    out = (tokens.astype(F32) + mixture).astype(BF)
    values = out.astype(F32)
    inverse_rms = lax.rsqrt(jnp.mean(values * values, axis=-1, keepdims=True) + 1e-06)
    normed = (values * inverse_rms * norm_gain.astype(F32)).astype(BF)
    projected = jnp.dot(
        normed,
        lax.all_gather(kv_weight, "grp", axis=1, tiled=True),
        preferred_element_type=F32,
    ).astype(BF)
    return (out[:rows], projected[:rows], out[rows:], projected[rows:], in_new[None], out_new[None])


def solution(mesh):
    split = P(("grp", "ep"), None)
    return jax.shard_map(
        local,
        mesh=mesh,
        in_specs=(split,) * 6 + (P(), P(), P("ep", None, None), P("ep", None, None), P(), P(None, "grp")),
        out_specs=(split,) * 4 + (P("ep", "grp", None), P("ep", None, "grp")),
        check_vma=False,
    )
```

```python
import jax
import jax.numpy as jnp
from jax import lax
from jax.experimental import pallas as pl
from jax.experimental.pallas import tpu as pltpu
from jax.sharding import PartitionSpec as P

TOP = 6
CHUNKS = 4
BF, F32 = jnp.bfloat16, jnp.float32
MESH = pl.DeviceIdType.MESH


def above(values, step, count):
    total = jnp.zeros_like(values)
    for i in range(1, count):
        total = total + (values >= i * step).astype(jnp.int32)
    return total


def iota(shape, dim):
    return lax.broadcasted_iota(jnp.int32, shape, dim)


def token_kernel(
    t1_ref, r1_ref, g1_ref, t2_ref, r2_ref, g2_ref, old_ref, new_ref, win_hbm, wout_hbm, gain_ref, kv_hbm,
    o_ref, kv_ref, in_new, out_new,
    kvw, acc, gainv, r1v, g1v, r2v, g2v, oldv, newv, srcv, srcs, mid_in, mid_out, pick_in, pick_out, fin_out,
    win, wout, ttab, tab, tabs, zbuf, pbuf, abuf, joined, rbuf, cbuf, sbuf, gbuf, own,
    wsem, lsem, tsend, trecv, zsend, zrecv, ysend, yrecv, rsend, rrecv, bsend, brecv,
    hsend, hrecv, fsend, frecv, selfsem, ksend, krecv,
):
    rows = t1_ref.shape[0]
    both = 2 * rows
    width = zbuf.shape[3]
    slab = pbuf.shape[2]
    cap = slab // 8
    inner = wout.shape[0]
    grp, ep = lax.axis_index("grp"), lax.axis_index("ep")
    x, low = grp % 4, grp // 4
    y, high, core = ep // 8, (ep // 2) % 4, ep % 2
    z = high * 2 + low
    sign = 1 - 2 * low
    me = y * 2 + core

    def at_z(step):
        there = (z + 8 + step) % 8
        return ((there % 2) * 4 + x, (y * 4 + there // 2) * 2 + core)

    def at_q(q):
        return (grp, ((q // 2) * 4 + high) * 2 + q % 2)

    z_to = (2 * sign, -3 * sign, -sign)
    z_from = (-2 * sign, -3 * sign, -sign)

    copies = [
        pltpu.make_async_copy(r1_ref, r1v, lsem.at[0]),
        pltpu.make_async_copy(g1_ref, g1v, lsem.at[1]),
        pltpu.make_async_copy(r2_ref, r2v, lsem.at[2]),
        pltpu.make_async_copy(g2_ref, g2v, lsem.at[3]),
        pltpu.make_async_copy(old_ref, oldv, lsem.at[7]),
        pltpu.make_async_copy(new_ref, newv, lsem.at[8]),
        pltpu.make_async_copy(gain_ref, gainv, lsem.at[9]),
    ]
    for copy in copies:
        copy.start()

    def place_copy(k, b):
        t_ref = t1_ref if b == 0 else t2_ref
        return pltpu.make_async_copy(
            t_ref.at[:, pl.ds(pl.multiple_of(k * width, width), width)], zbuf.at[k, 0, pl.ds(b * rows, rows)],
            lsem.at[4 + b])

    for k in range(CHUNKS):
        for b in range(2):
            place_copy(k, b).start()
    win_copy = pltpu.make_async_copy(win_hbm.at[0], win, wsem.at[0])
    wout_copy = pltpu.make_async_copy(wout_hbm.at[0], wout, wsem.at[1])
    win_copy.start()
    wout_copy.start()

    def at_ep(e):
        return (grp, e)

    barrier = pltpu.get_barrier_semaphore()
    for step in (2, -2, -3 * sign, -sign):
        pl.semaphore_signal(barrier, inc=1, device_id=at_z(step), device_id_type=MESH)

    def greet(off, carry):
        pl.semaphore_signal(barrier, inc=1, device_id=at_ep((ep + off) % 32), device_id_type=MESH)
        return carry

    lax.fori_loop(1, 32, greet, 0)

    def greet_grp(off, carry):
        pl.semaphore_signal(barrier, inc=1, device_id=((grp + off) % 8, ep), device_id_type=MESH)
        return carry

    lax.fori_loop(1, 8, greet_grp, 0)

    for copy in copies:
        copy.wait()
    square = (32, 32)

    def named_and_gates(r_ref, g_ref):
        named = jnp.zeros((32, rows), F32)
        gate = jnp.zeros((32, rows), F32)
        number = iota((32, rows), 0)
        for k in range(TOP):
            hit = r_ref[k:k + 1, :] == number
            named = named + jnp.where(hit, 1.0, 0.0)
            gate = gate + jnp.where(hit, g_ref[k:k + 1, :].astype(F32), 0.0)
        return named, gate

    diagonal = iota(square, 0) == iota(square, 1)
    old_column = jnp.sum(jnp.where(diagonal, oldv[...].astype(F32), 0.0), axis=1, keepdims=True)
    same = (old_column == newv[...].astype(F32)).astype(F32)
    found_at = jnp.sum(same * iota(square, 0).astype(F32), axis=0, keepdims=True)
    srcv[:, :32] = found_at.astype(jnp.int32)
    src_copy = pltpu.make_async_copy(srcv, srcs, lsem.at[6])
    src_copy.start()
    same = same.astype(BF)
    n1, gate1 = named_and_gates(r1v, g1v)
    n2, gate2 = named_and_gates(r2v, g2v)
    n2 = jnp.dot(same, n2.astype(BF), preferred_element_type=F32)
    gate2 = jnp.dot(same, gate2.astype(BF), preferred_element_type=F32)
    earlier = (iota((rows, rows), 0) < iota((rows, rows), 1)).astype(F32).astype(BF)

    def entries(named, offset):
        rank = jnp.dot(named.astype(BF), earlier, preferred_element_type=F32)
        return jnp.where(named > 0.5, rank + offset, -1.0)

    ttab[...] = jnp.zeros_like(ttab)
    ttab[:32, :rows] = entries(n1, 0.0)
    ttab[:32, rows:both] = entries(n2, float(cap))
    ttab[32:64, :rows] = gate1
    ttab[32:64, rows:both] = gate2
    tab[...] = jnp.transpose(ttab[...])[:both].astype(BF)
    tabs[0] = tab[...]
    for b in range(2):
        for k in range(CHUNKS):
            place_copy(k, b).wait()
    pl.semaphore_wait(barrier, 42)

    def part_in(j):
        return win_hbm.at[0, pl.ds(pl.multiple_of(grp * 256 + j * 8, 8), 8), :]

    def part_out(j):
        p = j // 2
        return wout_hbm.at[
            0, pl.ds(pl.multiple_of(8 * ((11 * p) // 2), 8), 48),
            pl.ds(pl.multiple_of(grp * 256 + (j % 2) * 128, 128), 128)]

    def ep_of(dy, dz, dc):
        return (((y + dy) % 4) * 4 + (high + dz) % 4) * 2 + (core + dc) % 2

    def ep_at(n, back):
        dy, dz, dc = (n // 2) % 4, n // 8, n % 2
        if back:
            return ep_of(4 - dy, 4 - dz, dc)
        return ep_of(dy, dz, dc)

    def spread_copies(n):
        j = ep_at(n, False)
        return [
            pltpu.make_async_remote_copy(
                src_ref=part_in(j), dst_ref=mid_in.at[ep], send_sem=hsend.at[0, n], recv_sem=hrecv.at[0, n],
                device_id=at_ep(j), device_id_type=MESH),
            pltpu.make_async_remote_copy(
                src_ref=part_out(j), dst_ref=mid_out.at[ep], send_sem=hsend.at[1, n], recv_sem=hrecv.at[1, n],
                device_id=at_ep(j), device_id_type=MESH)]

    def fetch_copies(n):
        s = ep_at(n, False)
        return [
            pltpu.make_async_remote_copy(
                src_ref=pick_in.at[s], dst_ref=in_new.at[pl.ds(pl.multiple_of(ep * 8, 8), 8), :],
                send_sem=fsend.at[0, n], recv_sem=frecv.at[0, n],
                device_id=at_ep(s), device_id_type=MESH),
            pltpu.make_async_remote_copy(
                src_ref=pick_out.at[s], dst_ref=fin_out.at[ep], send_sem=fsend.at[1, n], recv_sem=frecv.at[1, n],
                device_id=at_ep(s), device_id_type=MESH)]

    def start_spread(n, carry):
        for copy in spread_copies(n):
            copy.start()
        return carry

    def wait_spread(n, carry):
        for copy in spread_copies(n):
            copy.wait_recv()
        return carry

    own_spread = [
        pltpu.make_async_copy(part_in(ep), mid_in.at[ep], selfsem.at[0]),
        pltpu.make_async_copy(part_out(ep), mid_out.at[ep], selfsem.at[1])]
    own_fetch = [
        pltpu.make_async_copy(pick_in.at[ep], in_new.at[pl.ds(pl.multiple_of(ep * 8, 8), 8), :], selfsem.at[2]),
        pltpu.make_async_copy(pick_out.at[ep], fin_out.at[ep], selfsem.at[3])]

    def tab_copy(m):
        return pltpu.make_async_remote_copy(
            src_ref=tab, dst_ref=tabs.at[m + 1], send_sem=tsend.at[m], recv_sem=trecv.at[m],
            device_id=at_z(z_to[m]), device_id_type=MESH)

    def z_copy(k, m):
        return pltpu.make_async_remote_copy(
            src_ref=zbuf.at[k, 0], dst_ref=zbuf.at[k, m + 1], send_sem=zsend.at[k, m], recv_sem=zrecv.at[k, m],
            device_id=at_z(z_to[m]), device_id_type=MESH)

    def y_copy(k, off):
        q = (me + off) % 8
        return pltpu.make_async_remote_copy(
            src_ref=pbuf.at[k, q], dst_ref=abuf.at[k, me], send_sem=ysend.at[k, off], recv_sem=yrecv.at[k, off],
            device_id=at_q(q), device_id_type=MESH)

    def r_copy(k, off):
        q = (me + 8 - off) % 8
        return pltpu.make_async_remote_copy(
            src_ref=rbuf.at[k, q], dst_ref=cbuf.at[k, me], send_sem=rsend.at[k, off], recv_sem=rrecv.at[k, off],
            device_id=at_q(q), device_id_type=MESH)

    def b_copy(k, m):
        return pltpu.make_async_remote_copy(
            src_ref=sbuf.at[k, m], dst_ref=gbuf.at[k, m], send_sem=bsend.at[k, m], recv_sem=brecv.at[k, m],
            device_id=at_z(z_from[m]), device_id_type=MESH)

    for m in range(3):
        tab_copy(m).start()

    def send_z(k, carry):
        for m in range(3):
            z_copy(k, m).start()
        return carry

    lax.fori_loop(0, CHUNKS, send_z, 0)
    for copy in own_spread:
        copy.start()
    lax.fori_loop(1, 8, start_spread, 0)
    for m in range(3):
        tab_copy(m).wait_recv()

    half = kvw.shape[0] // 2
    kvw_cols = kv_hbm.shape[1]
    half_rows = pl.ds(pl.multiple_of(core * half, 8), half)
    grp_cols = pl.ds(pl.multiple_of(grp * kvw_cols, 128), kvw_cols)

    def kv_copy(off):
        return pltpu.make_async_remote_copy(
            src_ref=kv_hbm.at[half_rows, :], dst_ref=kvw.at[half_rows, grp_cols],
            send_sem=ksend.at[off], recv_sem=krecv.at[off],
            device_id=((grp + off) % 8, ep), device_id_type=MESH)

    kv_own = pltpu.make_async_copy(kv_hbm.at[half_rows, :], kvw.at[half_rows, grp_cols], selfsem.at[4])
    kv_swap = pltpu.make_async_remote_copy(
        src_ref=kvw.at[half_rows, :], dst_ref=kvw.at[half_rows, :], send_sem=ksend.at[0], recv_sem=krecv.at[0],
        device_id=at_q(y * 2 + 1 - core), device_id_type=MESH)

    def kv_start(off, carry):
        kv_copy(off).start()
        return carry

    def kv_wait(off, carry):
        kv_copy(off).wait_recv()
        return carry

    def kv_sent(off, carry):
        kv_copy(off).wait_send()
        return carry

    kv_own.start()
    lax.fori_loop(1, 8, kv_start, 0)

    total = 8 * slab
    gathered = 4 * both
    table = tabs[...].reshape(gathered, 128)

    def expert_of(q):
        return (q // 2) * 8 + high * 2 + q % 2

    def slot_facts(shape, dim):
        n = iota(shape, dim)
        q = above(n, slab, 8)
        inside = n - q * slab
        j = above(inside, 2 * cap, 4)
        half = above(q, 2, 4)
        return half * 8 + high * 2 + (q - 2 * half), j, (inside - j * 2 * cap).astype(F32)

    e_row, _, _ = slot_facts((total, 128), 0)
    choose = (iota((total, 128), 1) == e_row).astype(F32).astype(BF)
    found = lax.dot_general(choose, table, (((1,), (1,)), ((), ())), preferred_element_type=F32)
    _, j_row, r_row = slot_facts((total, gathered), 0)
    pick = ((found == r_row) & (j_row == above(iota((total, gathered), 1), both, 4))).astype(F32).astype(BF)
    e_col, _, _ = slot_facts((128, total), 1)
    choose_v = (iota((128, total), 0) == e_col).astype(F32).astype(BF)
    choose_g = (iota((128, total), 0) == e_col + 32).astype(F32).astype(BF)
    found_v = jnp.dot(table, choose_v, preferred_element_type=F32)
    found_g = jnp.dot(table, choose_g, preferred_element_type=F32)
    _, j_col, r_col = slot_facts((gathered, total), 1)
    mix = jnp.where(
        (found_v == r_col) & (j_col == above(iota((gathered, total), 0), both, 4)), found_g, 0.0).astype(BF)

    def pack(k, carry):
        for m in range(3):
            z_copy(k, m).wait_recv()
        packed = jnp.dot(pick, zbuf[k].reshape(gathered, width), preferred_element_type=F32)
        pbuf[k] = packed.reshape(8, slab, width).astype(BF)
        for off in range(1, 8):
            y_copy(k, off).start()
        abuf[k, me] = pbuf[k, me]
        return carry

    lax.fori_loop(0, CHUNKS, pack, 0)
    lax.fori_loop(8, 32, start_spread, 0)
    win_copy.wait()
    joined[...] = jnp.zeros_like(joined)

    def project(k, carry):
        for off in range(1, 8):
            y_copy(k, off).wait_recv()
        block = abuf[k].reshape(total, width)
        joined[...] += jnp.dot(
            block, win[pl.ds(pl.multiple_of(k * width, width), width), :], preferred_element_type=F32)
        return carry

    lax.fori_loop(0, CHUNKS, project, 0)
    gate_part = joined[:, :inner]
    hidden = (gate_part / (1.0 + jnp.exp(-gate_part)) * joined[:, inner:]).astype(BF)
    wout_copy.wait()

    def expand(k, carry):
        result = jnp.dot(
            hidden, wout[:, pl.ds(pl.multiple_of(k * width, width), width)], preferred_element_type=F32)
        rbuf[k] = result.reshape(8, slab, width).astype(BF)
        for off in range(1, 8):
            r_copy(k, off).start()
        cbuf[k, me] = rbuf[k, me]
        return carry

    lax.fori_loop(0, CHUNKS, expand, 0)

    kv_own.wait()
    lax.fori_loop(1, 8, kv_wait, 0)
    kv_swap.start()
    src_copy.wait()
    for copy in own_spread:
        copy.wait()
    lax.fori_loop(1, 32, wait_spread, 0)

    def choose_parts(s, carry):
        wanted = jnp.minimum(jnp.maximum(srcs[0, s], 0), 31)
        pick_in[s] = mid_in[wanted]
        pick_out[s] = mid_out[wanted]
        return carry

    lax.fori_loop(0, 32, choose_parts, 0)

    def start_fetch(n, carry):
        for copy in fetch_copies(n):
            copy.start()
        return carry

    lax.fori_loop(1, 32, start_fetch, 0)
    for copy in own_fetch:
        copy.start()

    def combine(k, carry):
        for off in range(1, 8):
            r_copy(k, off).wait_recv()
        part = jnp.dot(mix, cbuf[k].reshape(total, width), preferred_element_type=F32)
        own[k] = part[:both]
        sbuf[k] = part[both:].reshape(3, both, width).astype(BF)
        for m in range(3):
            b_copy(k, m).start()
        return carry

    lax.fori_loop(0, CHUNKS, combine, 0)

    kv_swap.wait()
    acc[...] = jnp.zeros_like(acc)

    def finish(k, squares):
        for m in range(3):
            b_copy(k, m).wait_recv()
        sums = own[k]
        for m in range(3):
            sums = sums + gbuf[k, m].astype(F32)
        columns = pl.ds(pl.multiple_of(k * width, width), width)
        after = (zbuf[k, 0].astype(F32) + sums).astype(BF)
        o_ref[:, columns] = after
        values = after.astype(F32)
        acc[...] += jnp.dot(
            (values * gainv[:, columns].astype(F32)).astype(BF), kvw[columns, :], preferred_element_type=F32)
        return squares + jnp.sum(values * values, axis=1, keepdims=True)

    squares = lax.fori_loop(0, CHUNKS, finish, jnp.zeros((both, 1), F32))
    kv_ref[...] = (acc[...] * lax.rsqrt(squares / (CHUNKS * width) + 1e-06)).astype(BF)
    lax.fori_loop(1, 8, kv_sent, 0)
    def end_fetch(n, carry):
        for copy in spread_copies(n):
            copy.wait_send()
        for copy in fetch_copies(n):
            copy.wait_send()
            copy.wait_recv()
        return carry

    for copy in own_fetch:
        copy.wait()
    lax.fori_loop(1, 32, end_fetch, 0)
    for p in range(16):
        first, count = 8 * ((11 * p) // 2), 40 + 8 * (p % 2)
        for h in range(2):
            out_new[first:first + count, 128 * h:128 * h + 128] = fin_out[2 * p + h, :count]
    for m in range(3):
        tab_copy(m).wait_send()

    def drain(k, carry):
        for m in range(3):
            z_copy(k, m).wait_send()
            b_copy(k, m).wait_send()
        for off in range(1, 8):
            y_copy(k, off).wait_send()
            r_copy(k, off).wait_send()
        return carry

    lax.fori_loop(0, CHUNKS, drain, 0)


def routed(t1, r1, g1, t2, r2, g2, old_table, new_table, gate_up, down_proj, gain, kv_weight):
    rows, features = t1.shape
    both = 2 * rows
    inner = down_proj.shape[1]
    experts = old_table.shape[0]
    cap = 3 * rows * TOP // (2 * experts)
    slab = 8 * cap
    width = features // CHUNKS
    vmem = pl.BlockSpec(memory_space=pltpu.VMEM)
    hbm = pl.BlockSpec(memory_space=pltpu.HBM)
    dma = pltpu.SemaphoreType.DMA
    part = features // 8
    return pl.pallas_call(
        token_kernel,
        out_shape=(
            jax.ShapeDtypeStruct((both, features), BF),
            jax.ShapeDtypeStruct((both, 8 * kv_weight.shape[1]), BF),
            jax.ShapeDtypeStruct((part, 2 * inner), BF),
            jax.ShapeDtypeStruct((inner, part), BF),
        ),
        in_specs=[hbm] * 12,
        out_specs=(vmem, vmem, hbm, vmem),
        scratch_shapes=[
            pltpu.VMEM((features, 8 * kv_weight.shape[1]), BF),
            pltpu.VMEM((both, 8 * kv_weight.shape[1]), F32),
            pltpu.VMEM((1, features), BF),
            pltpu.VMEM((TOP, rows), jnp.int32),
            pltpu.VMEM((TOP, rows), BF),
            pltpu.VMEM((TOP, rows), jnp.int32),
            pltpu.VMEM((TOP, rows), BF),
            pltpu.VMEM((1, 32), jnp.int32),
            pltpu.VMEM((1, 32), jnp.int32),
            pltpu.VMEM((1, 128), jnp.int32),
            pltpu.SMEM((1, 128), jnp.int32),
            pltpu.VMEM((32, 8, 2 * inner), BF),
            pltpu.VMEM((32, 48, 128), BF),
            pltpu.VMEM((32, 8, 2 * inner), BF),
            pltpu.VMEM((32, 48, 128), BF),
            pltpu.VMEM((32, 48, 128), BF),
            pltpu.VMEM((features, 2 * inner), BF),
            pltpu.VMEM((inner, features), BF),
            pltpu.VMEM((128, 128), F32),
            pltpu.VMEM((both, 128), BF),
            pltpu.VMEM((4, both, 128), BF),
            pltpu.VMEM((CHUNKS, 4, both, width), BF),
            pltpu.VMEM((CHUNKS, 8, slab, width), BF),
            pltpu.VMEM((CHUNKS, 8, slab, width), BF),
            pltpu.VMEM((8 * slab, 2 * inner), F32),
            pltpu.VMEM((CHUNKS, 8, slab, width), BF),
            pltpu.VMEM((CHUNKS, 8, slab, width), BF),
            pltpu.VMEM((CHUNKS, 3, both, width), BF),
            pltpu.VMEM((CHUNKS, 3, both, width), BF),
            pltpu.VMEM((CHUNKS, both, width), F32),
            dma((2,)), dma((10,)), dma((3,)), dma((3,)),
            dma((CHUNKS, 3)), dma((CHUNKS, 3)),
            dma((CHUNKS, 8)), dma((CHUNKS, 8)),
            dma((CHUNKS, 8)), dma((CHUNKS, 8)),
            dma((CHUNKS, 3)), dma((CHUNKS, 3)),
            dma((2, 32)), dma((2, 32)), dma((2, 32)), dma((2, 32)), dma((5,)), dma((8,)), dma((8,)),
        ],
        compiler_params=pltpu.CompilerParams(
            collective_id=0, has_side_effects=True, vmem_limit_bytes=60 << 20),
        cost_estimate=pl.CostEstimate(flops=8_000_000_000, bytes_accessed=200_000_000, transcendentals=0),
        name="routed_tokens",
    )(t1, r1.T, g1.T, t2, r2.T, g2.T, old_table[None, :], new_table[None, :], gate_up, down_proj,
      gain[None, :], kv_weight)


def local(
    tokens_one,
    routes_one,
    gates_one,
    tokens_two,
    routes_two,
    gates_two,
    old_table,
    new_table,
    gate_up,
    down_proj,
    norm_gain,
    kv_weight,
):
    rows = tokens_one.shape[0]
    hidden, kv, in_new, out_new = routed(
        tokens_one, routes_one, gates_one, tokens_two, routes_two, gates_two, old_table, new_table,
        gate_up, down_proj, norm_gain, kv_weight)
    return (hidden[:rows], kv[:rows], hidden[rows:], kv[rows:], in_new[None], out_new[None])


def solution(mesh):
    split = P(("grp", "ep"), None)
    return jax.shard_map(
        local,
        mesh=mesh,
        in_specs=(split,) * 6 + (P(), P(), P("ep", None, None), P("ep", None, None), P(), P(None, "grp")),
        out_specs=(split,) * 4 + (P("ep", "grp", None), P("ep", None, "grp")),
        check_vma=False,
    )
```

```python
import jax
import jax.numpy as jnp
from jax import lax
from jax.experimental import pallas as pl
from jax.experimental.pallas import tpu as pltpu
from jax.sharding import PartitionSpec as P

TOP = 6
CHUNKS = 4
BF, F32 = jnp.bfloat16, jnp.float32
MESH = pl.DeviceIdType.MESH


def above(values, step, count):
    total = jnp.zeros_like(values)
    for i in range(1, count):
        total = total + (values >= i * step).astype(jnp.int32)
    return total


def iota(shape, dim):
    return lax.broadcasted_iota(jnp.int32, shape, dim)


def token_kernel(
    t1_ref, r1_ref, g1_ref, t2_ref, r2_ref, g2_ref, old_ref, new_ref, win_hbm, wout_hbm, gain_ref, kv_hbm,
    o_ref, kv_ref, in_new, out_new,
    kvw, acc, gainv, gains, r1v, g1v, r2v, g2v, oldv, newv, srcv, srcs, mid_in, mid_out, pick_in, pick_out, fin_out,
    win, wout, ttab, tab, tabs, zbuf, pbuf, abuf, joined, rbuf, cbuf, sbuf, gbuf, own, third,
    wsem, lsem, tsend, trecv, zsend, zrecv, ysend, yrecv, rsend, rrecv, bsend, brecv,
    hsend, hrecv, fsend, frecv, selfsem, ksend, krecv,
):
    rows = t1_ref.shape[0]
    both = 2 * rows
    width = zbuf.shape[3]
    slab = pbuf.shape[2]
    cap = slab // 8
    inner = wout.shape[0]
    grp, ep = lax.axis_index("grp"), lax.axis_index("ep")
    x, low = grp % 4, grp // 4
    y, high, core = ep // 8, (ep // 2) % 4, ep % 2
    z = high * 2 + low
    sign = 1 - 2 * low
    me = y * 2 + core

    def at_z(step):
        there = (z + 8 + step) % 8
        return ((there % 2) * 4 + x, (y * 4 + there // 2) * 2 + core)

    def at_q(q):
        return (grp, ((q // 2) * 4 + high) * 2 + q % 2)

    z_to = (2 * sign, -3 * sign, -sign)

    copies = [
        pltpu.make_async_copy(r1_ref, r1v, lsem.at[0]),
        pltpu.make_async_copy(g1_ref, g1v, lsem.at[1]),
        pltpu.make_async_copy(r2_ref, r2v, lsem.at[2]),
        pltpu.make_async_copy(g2_ref, g2v, lsem.at[3]),
        pltpu.make_async_copy(old_ref, oldv, lsem.at[7]),
        pltpu.make_async_copy(new_ref, newv, lsem.at[8]),
        pltpu.make_async_copy(gain_ref, gainv, lsem.at[9]),
    ]
    for copy in copies:
        copy.start()

    def place_copy(k, b):
        t_ref = t1_ref if b == 0 else t2_ref
        return pltpu.make_async_copy(
            t_ref.at[:, pl.ds(pl.multiple_of(k * width, width), width)], zbuf.at[k, 0, pl.ds(b * rows, rows)],
            lsem.at[4 + b])

    for k in range(CHUNKS):
        for b in range(2):
            place_copy(k, b).start()
    win_copy = pltpu.make_async_copy(win_hbm.at[0], win, wsem.at[0])
    wout_copy = pltpu.make_async_copy(wout_hbm.at[0], wout, wsem.at[1])
    win_copy.start()
    wout_copy.start()

    def at_ep(e):
        return (grp, e)

    barrier = pltpu.get_barrier_semaphore()
    for step in (2, -2, -3 * sign, -sign):
        pl.semaphore_signal(barrier, inc=1, device_id=at_z(step), device_id_type=MESH)

    def greet(off, carry):
        pl.semaphore_signal(barrier, inc=1, device_id=at_ep((ep + off) % 32), device_id_type=MESH)
        return carry

    lax.fori_loop(1, 32, greet, 0)

    def greet_grp(off, carry):
        pl.semaphore_signal(barrier, inc=1, device_id=((grp + off) % 8, ep), device_id_type=MESH)
        return carry

    lax.fori_loop(1, 8, greet_grp, 0)

    for copy in copies:
        copy.wait()
    gains[...] = gainv[...].astype(F32)
    square = (32, 32)

    def named_and_gates(r_ref, g_ref):
        named = jnp.zeros((32, rows), F32)
        gate = jnp.zeros((32, rows), F32)
        number = iota((32, rows), 0)
        for k in range(TOP):
            hit = r_ref[k:k + 1, :] == number
            named = named + jnp.where(hit, 1.0, 0.0)
            gate = gate + jnp.where(hit, g_ref[k:k + 1, :].astype(F32), 0.0)
        return named, gate

    diagonal = iota(square, 0) == iota(square, 1)
    old_column = jnp.sum(jnp.where(diagonal, oldv[...].astype(F32), 0.0), axis=1, keepdims=True)
    same = (old_column == newv[...].astype(F32)).astype(F32)
    found_at = jnp.sum(same * iota(square, 0).astype(F32), axis=0, keepdims=True)
    srcv[:, :32] = found_at.astype(jnp.int32)
    src_copy = pltpu.make_async_copy(srcv, srcs, lsem.at[6])
    src_copy.start()
    same = same.astype(BF)
    n1, gate1 = named_and_gates(r1v, g1v)
    n2, gate2 = named_and_gates(r2v, g2v)
    n2 = jnp.dot(same, n2.astype(BF), preferred_element_type=F32)
    gate2 = jnp.dot(same, gate2.astype(BF), preferred_element_type=F32)
    earlier = (iota((rows, rows), 0) < iota((rows, rows), 1)).astype(F32).astype(BF)

    def entries(named, offset):
        rank = jnp.dot(named.astype(BF), earlier, preferred_element_type=F32)
        return jnp.where(named > 0.5, rank + offset, -1.0)

    ttab[...] = jnp.zeros_like(ttab)
    ttab[:32, :rows] = entries(n1, 0.0)
    ttab[:32, rows:both] = entries(n2, float(cap))
    ttab[32:64, :rows] = gate1
    ttab[32:64, rows:both] = gate2
    tab[...] = jnp.transpose(ttab[...])[:both].astype(BF)
    tabs[0] = tab[...]
    for b in range(2):
        for k in range(CHUNKS):
            place_copy(k, b).wait()
    pl.semaphore_wait(barrier, 42)

    def part_in(j):
        return win_hbm.at[0, pl.ds(pl.multiple_of(grp * 256 + j * 8, 8), 8), :]

    def part_out(j):
        p = j // 2
        return wout_hbm.at[
            0, pl.ds(pl.multiple_of(8 * ((11 * p) // 2), 8), 48),
            pl.ds(pl.multiple_of(grp * 256 + (j % 2) * 128, 128), 128)]

    def ep_of(dy, dz, dc):
        return (((y + dy) % 4) * 4 + (high + dz) % 4) * 2 + (core + dc) % 2

    def ep_at(n, back):
        dy, dz, dc = (n // 2) % 4, n // 8, n % 2
        if back:
            return ep_of(4 - dy, 4 - dz, dc)
        return ep_of(dy, dz, dc)

    def spread_copies(n):
        j = ep_at(n, False)
        return [
            pltpu.make_async_remote_copy(
                src_ref=part_in(j), dst_ref=mid_in.at[ep], send_sem=hsend.at[0, n], recv_sem=hrecv.at[0, n],
                device_id=at_ep(j), device_id_type=MESH),
            pltpu.make_async_remote_copy(
                src_ref=part_out(j), dst_ref=mid_out.at[ep], send_sem=hsend.at[1, n], recv_sem=hrecv.at[1, n],
                device_id=at_ep(j), device_id_type=MESH)]

    def fetch_copies(n):
        s = ep_at(n, False)
        return [
            pltpu.make_async_remote_copy(
                src_ref=pick_in.at[s], dst_ref=in_new.at[pl.ds(pl.multiple_of(ep * 8, 8), 8), :],
                send_sem=fsend.at[0, n], recv_sem=frecv.at[0, n],
                device_id=at_ep(s), device_id_type=MESH),
            pltpu.make_async_remote_copy(
                src_ref=pick_out.at[s], dst_ref=fin_out.at[ep], send_sem=fsend.at[1, n], recv_sem=frecv.at[1, n],
                device_id=at_ep(s), device_id_type=MESH)]

    def start_spread(n, carry):
        for copy in spread_copies(n):
            copy.start()
        return carry

    def wait_spread(n, carry):
        for copy in spread_copies(n):
            copy.wait_recv()
        return carry

    own_spread = [
        pltpu.make_async_copy(part_in(ep), mid_in.at[ep], selfsem.at[0]),
        pltpu.make_async_copy(part_out(ep), mid_out.at[ep], selfsem.at[1])]
    own_fetch = [
        pltpu.make_async_copy(pick_in.at[ep], in_new.at[pl.ds(pl.multiple_of(ep * 8, 8), 8), :], selfsem.at[2]),
        pltpu.make_async_copy(pick_out.at[ep], fin_out.at[ep], selfsem.at[3])]

    def tab_copy(m):
        return pltpu.make_async_remote_copy(
            src_ref=tab, dst_ref=tabs.at[m + 1], send_sem=tsend.at[m], recv_sem=trecv.at[m],
            device_id=at_z(z_to[m]), device_id_type=MESH)

    def z_copy(k, m):
        return pltpu.make_async_remote_copy(
            src_ref=zbuf.at[k, 3 if m == 1 else 0], dst_ref=zbuf.at[k, m + 1],
            send_sem=zsend.at[k, m], recv_sem=zrecv.at[k, m],
            device_id=at_z(-sign if m == 2 else 2 * sign), device_id_type=MESH)

    def y_copy(k, off):
        q = (me + off) % 8
        return pltpu.make_async_remote_copy(
            src_ref=pbuf.at[k, q], dst_ref=abuf.at[k, me], send_sem=ysend.at[k, off], recv_sem=yrecv.at[k, off],
            device_id=at_q(q), device_id_type=MESH)

    def r_copy(k, off):
        q = (me + 8 - off) % 8
        return pltpu.make_async_remote_copy(
            src_ref=rbuf.at[k, q], dst_ref=cbuf.at[k, me], send_sem=rsend.at[k, off], recv_sem=rrecv.at[k, off],
            device_id=at_q(q), device_id_type=MESH)

    def b_copy(k, m):
        return pltpu.make_async_remote_copy(
            src_ref=sbuf.at[k, m], dst_ref=gbuf.at[k, m], send_sem=bsend.at[k, m], recv_sem=brecv.at[k, m],
            device_id=at_z(-sign if m == 2 else -2 * sign), device_id_type=MESH)

    half = kvw.shape[0] // 2
    kvw_cols = kv_hbm.shape[1]
    half_rows = pl.ds(pl.multiple_of(core * half, 8), half)

    def kv_block(g):
        return kvw.at[half_rows, pl.ds(pl.multiple_of(g * kvw_cols, 128), kvw_cols)]

    def kv_copy(n):
        other = (grp + 4) % 8
        target = other if n == 4 else low * 4 + (x + n % 4) % 4
        return pltpu.make_async_remote_copy(
            src_ref=kv_block(other) if n > 4 else kv_hbm.at[half_rows, :],
            dst_ref=kv_block(other) if n > 4 else kv_block(grp),
            send_sem=ksend.at[n], recv_sem=krecv.at[n], device_id=(target, ep), device_id_type=MESH)

    kv_own = pltpu.make_async_copy(kv_hbm.at[half_rows, :], kv_block(grp), selfsem.at[4])
    kv_swap = pltpu.make_async_remote_copy(
        src_ref=kvw.at[half_rows, :], dst_ref=kvw.at[half_rows, :], send_sem=ksend.at[0], recv_sem=krecv.at[0],
        device_id=at_q(y * 2 + 1 - core), device_id_type=MESH)

    for m in range(3):
        tab_copy(m).start()
    for n in (4, 1, 2, 3):
        kv_copy(n).start()
    kv_own.start()

    def send_z(k, carry):
        for m in (2, 0):
            z_copy(k, m).start()
        return carry

    def hand_on(k):
        z_copy(k, 2).wait_recv()
        z_copy(k, 1).start()

    lax.fori_loop(0, CHUNKS, send_z, 0)
    for copy in own_spread:
        copy.start()
    lax.fori_loop(1, 8, start_spread, 0)
    for m in range(3):
        tab_copy(m).wait_recv()

    total = 8 * slab
    gathered = 4 * both
    table = tabs[...].reshape(gathered, 128)

    def expert_of(q):
        return (q // 2) * 8 + high * 2 + q % 2

    def slot_facts(shape, dim):
        n = iota(shape, dim)
        q = above(n, slab, 8)
        inside = n - q * slab
        j = above(inside, 2 * cap, 4)
        half = above(q, 2, 4)
        return half * 8 + high * 2 + (q - 2 * half), j, (inside - j * 2 * cap).astype(F32)

    e_row, _, _ = slot_facts((total, 128), 0)
    choose = (iota((total, 128), 1) == e_row).astype(F32).astype(BF)
    found = lax.dot_general(choose, table, (((1,), (1,)), ((), ())), preferred_element_type=F32)
    _, j_row, r_row = slot_facts((total, gathered), 0)
    pick = ((found == r_row) & (j_row == above(iota((total, gathered), 1), both, 4))).astype(F32).astype(BF)
    e_col, _, _ = slot_facts((128, total), 1)
    choose_v = (iota((128, total), 0) == e_col).astype(F32).astype(BF)
    choose_g = (iota((128, total), 0) == e_col + 32).astype(F32).astype(BF)
    found_v = jnp.dot(table, choose_v, preferred_element_type=F32)
    found_g = jnp.dot(table, choose_g, preferred_element_type=F32)
    _, j_col, r_col = slot_facts((gathered, total), 1)
    mix = jnp.where(
        (found_v == r_col) & (j_col == above(iota((gathered, total), 0), both, 4)), found_g, 0.0).astype(BF)

    kv_copy(4).wait_recv()
    for n in (5, 6, 7):
        kv_copy(n).start()

    hand_on(0)

    def pack(k, carry):
        @pl.when(k + 1 < CHUNKS)
        def _():
            hand_on(k + 1)

        for m in range(2):
            z_copy(k, m).wait_recv()
        packed = jnp.dot(pick, zbuf[k].reshape(gathered, width), preferred_element_type=F32)
        pbuf[k] = packed.reshape(8, slab, width).astype(BF)
        for off in range(1, 8):
            y_copy(k, off).start()
        abuf[k, me] = pbuf[k, me]
        return carry

    lax.fori_loop(0, CHUNKS, pack, 0)
    lax.fori_loop(8, 32, start_spread, 0)
    win_copy.wait()
    joined[...] = jnp.zeros_like(joined)

    def project(k, carry):
        for off in range(1, 8):
            y_copy(k, off).wait_recv()
        block = abuf[k].reshape(total, width)
        joined[...] += jnp.dot(
            block, win[pl.ds(pl.multiple_of(k * width, width), width), :], preferred_element_type=F32)
        return carry

    lax.fori_loop(0, CHUNKS, project, 0)
    gate_part = joined[:, :inner]
    hidden = (gate_part / (1.0 + jnp.exp(-gate_part)) * joined[:, inner:]).astype(BF)
    wout_copy.wait()

    def expand(k, carry):
        result = jnp.dot(
            hidden, wout[:, pl.ds(pl.multiple_of(k * width, width), width)], preferred_element_type=F32)
        rbuf[k] = result.reshape(8, slab, width).astype(BF)
        for off in range(1, 8):
            r_copy(k, off).start()
        cbuf[k, me] = rbuf[k, me]
        return carry

    lax.fori_loop(0, CHUNKS, expand, 0)

    kv_own.wait()
    for n in (1, 2, 3, 5, 6, 7):
        kv_copy(n).wait_recv()
    kv_swap.start()
    src_copy.wait()
    for copy in own_spread:
        copy.wait()
    lax.fori_loop(1, 32, wait_spread, 0)

    def choose_parts(s, carry):
        wanted = jnp.minimum(jnp.maximum(srcs[0, s], 0), 31)
        pick_in[s] = mid_in[wanted]
        pick_out[s] = mid_out[wanted]
        return carry

    lax.fori_loop(0, 32, choose_parts, 0)

    def start_fetch(n, carry):
        for copy in fetch_copies(n):
            copy.start()
        return carry

    lax.fori_loop(1, 32, start_fetch, 0)
    for copy in own_fetch:
        copy.start()

    def combine(k, carry):
        for off in range(1, 8):
            r_copy(k, off).wait_recv()
        part = jnp.dot(mix, cbuf[k].reshape(total, width), preferred_element_type=F32)
        own[k] = part[:both]
        third[k] = part[3 * both:]
        sbuf[k, 0] = part[both:2 * both].astype(BF)
        sbuf[k, 1] = part[2 * both:3 * both].astype(BF)
        for m in (1, 0):
            b_copy(k, m).start()

        @pl.when(k > 0)
        def _():
            fold(k - 1)

        return carry

    def fold(k):
        b_copy(k, 1).wait_recv()
        sbuf[k, 2] = (third[k] + gbuf[k, 1].astype(F32)).astype(BF)
        b_copy(k, 2).start()

    lax.fori_loop(0, CHUNKS, combine, 0)
    fold(CHUNKS - 1)

    kv_swap.wait()
    acc[...] = jnp.zeros_like(acc)

    def finish(k, squares):
        for m in (0, 2):
            b_copy(k, m).wait_recv()
        sums = own[k] + gbuf[k, 0].astype(F32) + gbuf[k, 2].astype(F32)
        columns = pl.ds(pl.multiple_of(k * width, width), width)
        after = (zbuf[k, 0].astype(F32) + sums).astype(BF)
        o_ref[:, columns] = after
        values = after.astype(F32)
        lines = width // 128
        gain = jnp.concatenate([gains[pl.ds(k * lines + i, 1), :] for i in range(lines)], axis=1)
        acc[...] += jnp.dot(
            (values * gain).astype(BF), kvw[columns, :], preferred_element_type=F32)
        return squares + jnp.sum(values * values, axis=1, keepdims=True)

    squares = lax.fori_loop(0, CHUNKS, finish, jnp.zeros((both, 1), F32))
    kv_ref[...] = (acc[...] * lax.rsqrt(squares / (CHUNKS * width) + 1e-06)).astype(BF)
    for n in range(1, 8):
        kv_copy(n).wait_send()
    def end_fetch(n, carry):
        for copy in spread_copies(n):
            copy.wait_send()
        for copy in fetch_copies(n):
            copy.wait_send()
            copy.wait_recv()
        return carry

    for copy in own_fetch:
        copy.wait()
    lax.fori_loop(1, 32, end_fetch, 0)
    for p in range(16):
        first, count = 8 * ((11 * p) // 2), 40 + 8 * (p % 2)
        for h in range(2):
            out_new[first:first + count, 128 * h:128 * h + 128] = fin_out[2 * p + h, :count]
    for m in range(3):
        tab_copy(m).wait_send()

    def drain(k, carry):
        for m in range(3):
            z_copy(k, m).wait_send()
            b_copy(k, m).wait_send()
        for off in range(1, 8):
            y_copy(k, off).wait_send()
            r_copy(k, off).wait_send()
        return carry

    lax.fori_loop(0, CHUNKS, drain, 0)


def routed(t1, r1, g1, t2, r2, g2, old_table, new_table, gate_up, down_proj, gain, kv_weight):
    rows, features = t1.shape
    both = 2 * rows
    inner = down_proj.shape[1]
    experts = old_table.shape[0]
    cap = 3 * rows * TOP // (2 * experts)
    slab = 8 * cap
    width = features // CHUNKS
    vmem = pl.BlockSpec(memory_space=pltpu.VMEM)
    hbm = pl.BlockSpec(memory_space=pltpu.HBM)
    dma = pltpu.SemaphoreType.DMA
    part = features // 8
    return pl.pallas_call(
        token_kernel,
        out_shape=(
            jax.ShapeDtypeStruct((both, features), BF),
            jax.ShapeDtypeStruct((both, 8 * kv_weight.shape[1]), BF),
            jax.ShapeDtypeStruct((part, 2 * inner), BF),
            jax.ShapeDtypeStruct((inner, part), BF),
        ),
        in_specs=[hbm] * 12,
        out_specs=(vmem, vmem, hbm, vmem),
        scratch_shapes=[
            pltpu.VMEM((features, 8 * kv_weight.shape[1]), BF),
            pltpu.VMEM((both, 8 * kv_weight.shape[1]), F32),
            pltpu.VMEM((features // 128, 128), BF),
            pltpu.VMEM((features // 128, 128), F32),
            pltpu.VMEM((TOP, rows), jnp.int32),
            pltpu.VMEM((TOP, rows), BF),
            pltpu.VMEM((TOP, rows), jnp.int32),
            pltpu.VMEM((TOP, rows), BF),
            pltpu.VMEM((1, 32), jnp.int32),
            pltpu.VMEM((1, 32), jnp.int32),
            pltpu.VMEM((1, 128), jnp.int32),
            pltpu.SMEM((1, 128), jnp.int32),
            pltpu.VMEM((32, 8, 2 * inner), BF),
            pltpu.VMEM((32, 48, 128), BF),
            pltpu.VMEM((32, 8, 2 * inner), BF),
            pltpu.VMEM((32, 48, 128), BF),
            pltpu.VMEM((32, 48, 128), BF),
            pltpu.VMEM((features, 2 * inner), BF),
            pltpu.VMEM((inner, features), BF),
            pltpu.VMEM((128, 128), F32),
            pltpu.VMEM((both, 128), BF),
            pltpu.VMEM((4, both, 128), BF),
            pltpu.VMEM((CHUNKS, 4, both, width), BF),
            pltpu.VMEM((CHUNKS, 8, slab, width), BF),
            pltpu.VMEM((CHUNKS, 8, slab, width), BF),
            pltpu.VMEM((8 * slab, 2 * inner), F32),
            pltpu.VMEM((CHUNKS, 8, slab, width), BF),
            pltpu.VMEM((CHUNKS, 8, slab, width), BF),
            pltpu.VMEM((CHUNKS, 3, both, width), BF),
            pltpu.VMEM((CHUNKS, 3, both, width), BF),
            pltpu.VMEM((CHUNKS, both, width), F32),
            pltpu.VMEM((CHUNKS, both, width), F32),
            dma((2,)), dma((10,)), dma((3,)), dma((3,)),
            dma((CHUNKS, 3)), dma((CHUNKS, 3)),
            dma((CHUNKS, 8)), dma((CHUNKS, 8)),
            dma((CHUNKS, 8)), dma((CHUNKS, 8)),
            dma((CHUNKS, 3)), dma((CHUNKS, 3)),
            dma((2, 32)), dma((2, 32)), dma((2, 32)), dma((2, 32)), dma((5,)), dma((8,)), dma((8,)),
        ],
        compiler_params=pltpu.CompilerParams(
            collective_id=0, has_side_effects=True, vmem_limit_bytes=60 << 20),
        cost_estimate=pl.CostEstimate(flops=8_000_000_000, bytes_accessed=200_000_000, transcendentals=0),
        name="routed_tokens",
    )(t1, r1.T, g1.T, t2, r2.T, g2.T, old_table[None, :], new_table[None, :], gate_up, down_proj,
      gain.reshape(features // 128, 128), kv_weight)


def hand_out(hid_ref, kv_ref, in_ref, out_ref, h1_ref, k1_ref, h2_ref, k2_ref, in_new, out_new, hid, kv, inv, outv, sems):
    rows = h1_ref.shape[0]
    first, second = pl.ds(0, rows), pl.ds(rows, rows)
    reads = [
        pltpu.make_async_copy(src, dst, sems.at[i])
        for i, (src, dst) in enumerate(((in_ref, inv), (out_ref, outv), (hid_ref, hid), (kv_ref, kv)))
    ]
    writes = [
        [(inv, in_new.at[0])], [(outv, out_new.at[0])],
        [(hid.at[first], h1_ref), (hid.at[second], h2_ref)], [(kv.at[first], k1_ref), (kv.at[second], k2_ref)],
    ]
    for copy in reads:
        copy.start()
    started = []
    for copy, targets in zip(reads, writes):
        copy.wait()
        for src, dst in targets:
            write = pltpu.make_async_copy(src, dst, sems.at[4 + len(started)])
            write.start()
            started.append(write)
    for write in started:
        write.wait()


def local(
    tokens_one,
    routes_one,
    gates_one,
    tokens_two,
    routes_two,
    gates_two,
    old_table,
    new_table,
    gate_up,
    down_proj,
    norm_gain,
    kv_weight,
):
    rows = tokens_one.shape[0]
    hidden, kv, in_new, out_new = routed(
        tokens_one, routes_one, gates_one, tokens_two, routes_two, gates_two, old_table, new_table,
        gate_up, down_proj, norm_gain, kv_weight)
    hbm = pl.BlockSpec(memory_space=pltpu.HBM)
    token_rows = jax.ShapeDtypeStruct((rows, hidden.shape[1]), BF)
    kv_rows = jax.ShapeDtypeStruct((rows, kv.shape[1]), BF)
    return pl.pallas_call(
        hand_out,
        out_shape=(
            token_rows, kv_rows, token_rows, kv_rows,
            jax.ShapeDtypeStruct((1,) + in_new.shape, BF), jax.ShapeDtypeStruct((1,) + out_new.shape, BF)),
        in_specs=[hbm] * 4,
        out_specs=(hbm,) * 6,
        scratch_shapes=[pltpu.VMEM(array.shape, BF) for array in (hidden, kv, in_new, out_new)]
        + [pltpu.SemaphoreType.DMA((10,))],
        compiler_params=pltpu.CompilerParams(vmem_limit_bytes=60 << 20),
        name="hand_out",
    )(hidden, kv, in_new, out_new)


def solution(mesh):
    split = P(("grp", "ep"), None)
    return jax.shard_map(
        local,
        mesh=mesh,
        in_specs=(split,) * 6 + (P(), P(), P("ep", None, None), P("ep", None, None), P(), P(None, "grp")),
        out_specs=(split,) * 4 + (P("ep", "grp", None), P("ep", None, "grp")),
        check_vma=False,
    )
```

```python
import jax
import jax.numpy as jnp
from jax import lax
from jax.experimental import pallas as pl
from jax.experimental.pallas import tpu as pltpu
from jax.sharding import PartitionSpec as P

TOP = 6
CHUNKS = 4
BF, F32 = jnp.bfloat16, jnp.float32
MESH = pl.DeviceIdType.MESH


def above(values, step, count):
    total = jnp.zeros_like(values)
    for i in range(1, count):
        total = total + (values >= i * step).astype(jnp.int32)
    return total


def iota(shape, dim):
    return lax.broadcasted_iota(jnp.int32, shape, dim)


def token_kernel(
    t1_ref, r1_ref, g1_ref, t2_ref, r2_ref, g2_ref, old_ref, new_ref, win_hbm, wout_hbm, gain_ref, kv_hbm,
    o_ref, kv_ref, in_new, out_new,
    kvw, acc, gainv, gains, r1v, g1v, r2v, g2v, oldv, newv, srcv, srcs, mid_in, mid_out, pick_in, pick_out, fin_out,
    win, wout, ttab, tab, tabs, zbuf, pbuf, abuf, joined, rbuf, cbuf, sbuf, gbuf, own, third,
    wsem, lsem, tsend, trecv, zsend, zrecv, ysend, yrecv, rsend, rrecv, bsend, brecv,
    hsend, hrecv, fsend, frecv, selfsem, ksend, krecv,
):
    rows = t1_ref.shape[0]
    both = 2 * rows
    width = zbuf.shape[3]
    slab = pbuf.shape[2]
    cap = slab // 8
    inner = wout.shape[0]
    grp, ep = lax.axis_index("grp"), lax.axis_index("ep")
    x, low = grp % 4, grp // 4
    y, high, core = ep // 8, (ep // 2) % 4, ep % 2
    z = high * 2 + low
    sign = 1 - 2 * low
    me = y * 2 + core

    def at_z(step):
        there = (z + 8 + step) % 8
        return ((there % 2) * 4 + x, (y * 4 + there // 2) * 2 + core)

    def at_q(q):
        return (grp, ((q // 2) * 4 + high) * 2 + q % 2)

    z_to = (2 * sign, -3 * sign, -sign)

    copies = [
        pltpu.make_async_copy(r1_ref, r1v, lsem.at[0]),
        pltpu.make_async_copy(g1_ref, g1v, lsem.at[1]),
        pltpu.make_async_copy(r2_ref, r2v, lsem.at[2]),
        pltpu.make_async_copy(g2_ref, g2v, lsem.at[3]),
        pltpu.make_async_copy(old_ref, oldv, lsem.at[7]),
        pltpu.make_async_copy(new_ref, newv, lsem.at[8]),
        pltpu.make_async_copy(gain_ref, gainv, lsem.at[9]),
    ]
    for copy in copies:
        copy.start()

    def place_copy(k, b):
        t_ref = t1_ref if b == 0 else t2_ref
        return pltpu.make_async_copy(
            t_ref.at[:, pl.ds(pl.multiple_of(k * width, width), width)], zbuf.at[k, 0, pl.ds(b * rows, rows)],
            lsem.at[4 + b])

    for k in range(CHUNKS):
        for b in range(2):
            place_copy(k, b).start()
    win_copy = pltpu.make_async_copy(win_hbm.at[0], win, wsem.at[0])
    wout_copy = pltpu.make_async_copy(wout_hbm.at[0], wout, wsem.at[1])
    win_copy.start()
    wout_copy.start()

    def at_ep(e):
        return (grp, e)

    barrier = pltpu.get_barrier_semaphore()
    for step in (2, -2, -3 * sign, -sign):
        pl.semaphore_signal(barrier, inc=1, device_id=at_z(step), device_id_type=MESH)

    def greet(off, carry):
        pl.semaphore_signal(barrier, inc=1, device_id=at_ep((ep + off) % 32), device_id_type=MESH)
        return carry

    lax.fori_loop(1, 32, greet, 0)

    def greet_grp(off, carry):
        pl.semaphore_signal(barrier, inc=1, device_id=((grp + off) % 8, ep), device_id_type=MESH)
        return carry

    lax.fori_loop(1, 8, greet_grp, 0)

    for copy in copies:
        copy.wait()
    gains[...] = gainv[...].astype(F32)
    square = (32, 32)

    def named_and_gates(r_ref, g_ref):
        named = jnp.zeros((32, rows), F32)
        gate = jnp.zeros((32, rows), F32)
        number = iota((32, rows), 0)
        for k in range(TOP):
            hit = r_ref[k:k + 1, :] == number
            named = named + jnp.where(hit, 1.0, 0.0)
            gate = gate + jnp.where(hit, g_ref[k:k + 1, :].astype(F32), 0.0)
        return named, gate

    diagonal = iota(square, 0) == iota(square, 1)
    old_column = jnp.sum(jnp.where(diagonal, oldv[...].astype(F32), 0.0), axis=1, keepdims=True)
    same = (old_column == newv[...].astype(F32)).astype(F32)
    found_at = jnp.sum(same * iota(square, 0).astype(F32), axis=0, keepdims=True)
    srcv[:, :32] = found_at.astype(jnp.int32)
    src_copy = pltpu.make_async_copy(srcv, srcs, lsem.at[6])
    src_copy.start()
    same = same.astype(BF)
    n1, gate1 = named_and_gates(r1v, g1v)
    n2, gate2 = named_and_gates(r2v, g2v)
    n2 = jnp.dot(same, n2.astype(BF), preferred_element_type=F32)
    gate2 = jnp.dot(same, gate2.astype(BF), preferred_element_type=F32)
    earlier = (iota((rows, rows), 0) < iota((rows, rows), 1)).astype(F32).astype(BF)

    def entries(named, offset):
        rank = jnp.dot(named.astype(BF), earlier, preferred_element_type=F32)
        return jnp.where(named > 0.5, rank + offset, -1.0)

    ttab[...] = jnp.zeros_like(ttab)
    ttab[:32, :rows] = entries(n1, 0.0)
    ttab[:32, rows:both] = entries(n2, float(cap))
    ttab[32:64, :rows] = gate1
    ttab[32:64, rows:both] = gate2
    tab[...] = jnp.transpose(ttab[...])[:both].astype(BF)
    tabs[0] = tab[...]
    for b in range(2):
        for k in range(CHUNKS):
            place_copy(k, b).wait()
    pl.semaphore_wait(barrier, 42)

    def part_in(j):
        return win_hbm.at[0, pl.ds(pl.multiple_of(grp * 256 + j * 8, 8), 8), :]

    def part_out(j):
        p = j // 2
        return wout_hbm.at[
            0, pl.ds(pl.multiple_of(8 * ((11 * p) // 2), 8), 48),
            pl.ds(pl.multiple_of(grp * 256 + (j % 2) * 128, 128), 128)]

    def ep_of(dy, dz, dc):
        return (((y + dy) % 4) * 4 + (high + dz) % 4) * 2 + (core + dc) % 2

    def ep_at(n, back):
        dy, dz, dc = n // 8, n % 4, (n // 4) % 2
        if back:
            return ep_of(4 - dy, 4 - dz, dc)
        return ep_of(dy, dz, dc)

    def spread_copies(n):
        j = ep_at(n, False)
        return [
            pltpu.make_async_remote_copy(
                src_ref=part_in(j), dst_ref=mid_in.at[ep], send_sem=hsend.at[0, n], recv_sem=hrecv.at[0, n],
                device_id=at_ep(j), device_id_type=MESH),
            pltpu.make_async_remote_copy(
                src_ref=part_out(j), dst_ref=mid_out.at[ep], send_sem=hsend.at[1, n], recv_sem=hrecv.at[1, n],
                device_id=at_ep(j), device_id_type=MESH)]

    def fetch_copies(n):
        s = ep_at(n, False)
        return [
            pltpu.make_async_remote_copy(
                src_ref=pick_in.at[s], dst_ref=in_new.at[pl.ds(pl.multiple_of(ep * 8, 8), 8), :],
                send_sem=fsend.at[0, n], recv_sem=frecv.at[0, n],
                device_id=at_ep(s), device_id_type=MESH),
            pltpu.make_async_remote_copy(
                src_ref=pick_out.at[s], dst_ref=fin_out.at[ep], send_sem=fsend.at[1, n], recv_sem=frecv.at[1, n],
                device_id=at_ep(s), device_id_type=MESH)]

    def start_spread(n, carry):
        for copy in spread_copies(n):
            copy.start()
        return carry

    def wait_spread(n, carry):
        for copy in spread_copies(n):
            copy.wait_recv()
        return carry

    own_spread = [
        pltpu.make_async_copy(part_in(ep), mid_in.at[ep], selfsem.at[0]),
        pltpu.make_async_copy(part_out(ep), mid_out.at[ep], selfsem.at[1])]
    own_fetch = [
        pltpu.make_async_copy(pick_in.at[ep], in_new.at[pl.ds(pl.multiple_of(ep * 8, 8), 8), :], selfsem.at[2]),
        pltpu.make_async_copy(pick_out.at[ep], fin_out.at[ep], selfsem.at[3])]

    def tab_copy(m):
        return pltpu.make_async_remote_copy(
            src_ref=tab, dst_ref=tabs.at[m + 1], send_sem=tsend.at[m], recv_sem=trecv.at[m],
            device_id=at_z(z_to[m]), device_id_type=MESH)

    def z_copy(k, m):
        return pltpu.make_async_remote_copy(
            src_ref=zbuf.at[k, 3 if m == 1 else 0], dst_ref=zbuf.at[k, m + 1],
            send_sem=zsend.at[k, m], recv_sem=zrecv.at[k, m],
            device_id=at_z(-sign if m == 2 else 2 * sign), device_id_type=MESH)

    def y_copy(k, off):
        q = (me + off) % 8
        return pltpu.make_async_remote_copy(
            src_ref=pbuf.at[k, q], dst_ref=abuf.at[k, me], send_sem=ysend.at[k, off], recv_sem=yrecv.at[k, off],
            device_id=at_q(q), device_id_type=MESH)

    def r_copy(k, off):
        q = (me + 8 - off) % 8
        return pltpu.make_async_remote_copy(
            src_ref=rbuf.at[k, q], dst_ref=cbuf.at[k, me], send_sem=rsend.at[k, off], recv_sem=rrecv.at[k, off],
            device_id=at_q(q), device_id_type=MESH)

    def b_copy(k, m):
        return pltpu.make_async_remote_copy(
            src_ref=sbuf.at[k, m], dst_ref=gbuf.at[k, m], send_sem=bsend.at[k, m], recv_sem=brecv.at[k, m],
            device_id=at_z(-sign if m == 2 else -2 * sign), device_id_type=MESH)

    half = kvw.shape[0] // 2
    kvw_cols = kv_hbm.shape[1]
    half_rows = pl.ds(pl.multiple_of(core * half, 8), half)

    def kv_block(g):
        return kvw.at[half_rows, pl.ds(pl.multiple_of(g * kvw_cols, 128), kvw_cols)]

    def kv_copy(n):
        other = (grp + 4) % 8
        target = other if n == 4 else low * 4 + (x + n % 4) % 4
        return pltpu.make_async_remote_copy(
            src_ref=kv_block(other) if n > 4 else kv_hbm.at[half_rows, :],
            dst_ref=kv_block(other) if n > 4 else kv_block(grp),
            send_sem=ksend.at[n], recv_sem=krecv.at[n], device_id=(target, ep), device_id_type=MESH)

    kv_own = pltpu.make_async_copy(kv_hbm.at[half_rows, :], kv_block(grp), selfsem.at[4])
    kv_swap = pltpu.make_async_remote_copy(
        src_ref=kvw.at[half_rows, :], dst_ref=kvw.at[half_rows, :], send_sem=ksend.at[0], recv_sem=krecv.at[0],
        device_id=at_q(y * 2 + 1 - core), device_id_type=MESH)

    for m in range(3):
        tab_copy(m).start()
    for n in (4, 1, 2, 3):
        kv_copy(n).start()
    kv_own.start()

    def send_z(k, carry):
        for m in (2, 0):
            z_copy(k, m).start()
        return carry

    def hand_on(k):
        z_copy(k, 2).wait_recv()
        z_copy(k, 1).start()

    lax.fori_loop(0, CHUNKS, send_z, 0)
    for copy in own_spread:
        copy.start()
    lax.fori_loop(1, 8, lambda n, carry: start_spread(n * 4, carry), 0)
    for m in range(3):
        tab_copy(m).wait_recv()

    total = 8 * slab
    gathered = 4 * both
    table = tabs[...].reshape(gathered, 128)

    def expert_of(q):
        return (q // 2) * 8 + high * 2 + q % 2

    def slot_facts(shape, dim):
        n = iota(shape, dim)
        q = above(n, slab, 8)
        inside = n - q * slab
        j = above(inside, 2 * cap, 4)
        half = above(q, 2, 4)
        return half * 8 + high * 2 + (q - 2 * half), j, (inside - j * 2 * cap).astype(F32)

    e_row, _, _ = slot_facts((total, 128), 0)
    choose = (iota((total, 128), 1) == e_row).astype(F32).astype(BF)
    found = lax.dot_general(choose, table, (((1,), (1,)), ((), ())), preferred_element_type=F32)
    _, j_row, r_row = slot_facts((total, gathered), 0)
    pick = ((found == r_row) & (j_row == above(iota((total, gathered), 1), both, 4))).astype(F32).astype(BF)
    e_col, _, _ = slot_facts((128, total), 1)
    choose_v = (iota((128, total), 0) == e_col).astype(F32).astype(BF)
    choose_g = (iota((128, total), 0) == e_col + 32).astype(F32).astype(BF)
    found_v = jnp.dot(table, choose_v, preferred_element_type=F32)
    found_g = jnp.dot(table, choose_g, preferred_element_type=F32)
    _, j_col, r_col = slot_facts((gathered, total), 1)
    mix = jnp.where(
        (found_v == r_col) & (j_col == above(iota((gathered, total), 0), both, 4)), found_g, 0.0).astype(BF)

    kv_copy(4).wait_recv()
    for n in (5, 6, 7):
        kv_copy(n).start()

    hand_on(0)

    def pack(k, carry):
        @pl.when(k + 1 < CHUNKS)
        def _():
            hand_on(k + 1)

        for m in range(2):
            z_copy(k, m).wait_recv()
        packed = jnp.dot(pick, zbuf[k].reshape(gathered, width), preferred_element_type=F32)
        pbuf[k] = packed.reshape(8, slab, width).astype(BF)
        for off in (2, 6, 4, 3, 7, 5, 1):
            y_copy(k, off).start()
        abuf[k, me] = pbuf[k, me]
        return carry

    lax.fori_loop(0, CHUNKS - 1, pack, 0)
    lax.fori_loop(0, 24, lambda i, carry: start_spread((i // 3) * 4 + i % 3 + 1, carry), 0)
    lax.fori_loop(CHUNKS - 1, CHUNKS, pack, 0)
    win_copy.wait()
    joined[...] = jnp.zeros_like(joined)

    def project(k, carry):
        for off in range(1, 8):
            y_copy(k, off).wait_recv()
        block = abuf[k].reshape(total, width)
        joined[...] += jnp.dot(
            block, win[pl.ds(pl.multiple_of(k * width, width), width), :], preferred_element_type=F32)
        return carry

    lax.fori_loop(0, CHUNKS, project, 0)
    gate_part = joined[:, :inner]
    hidden = (gate_part / (1.0 + jnp.exp(-gate_part)) * joined[:, inner:]).astype(BF)
    wout_copy.wait()

    def expand(k, carry):
        result = jnp.dot(
            hidden, wout[:, pl.ds(pl.multiple_of(k * width, width), width)], preferred_element_type=F32)
        rbuf[k] = result.reshape(8, slab, width).astype(BF)
        for off in (2, 6, 4, 3, 7, 5, 1):
            r_copy(k, off).start()
        cbuf[k, me] = rbuf[k, me]
        return carry

    lax.fori_loop(0, CHUNKS, expand, 0)

    kv_own.wait()
    for n in (1, 2, 3, 5, 6, 7):
        kv_copy(n).wait_recv()
    kv_swap.start()
    src_copy.wait()
    for copy in own_spread:
        copy.wait()
    lax.fori_loop(1, 32, wait_spread, 0)

    def choose_parts(s, carry):
        wanted = jnp.minimum(jnp.maximum(srcs[0, s], 0), 31)
        pick_in[s] = mid_in[wanted]
        pick_out[s] = mid_out[wanted]
        return carry

    lax.fori_loop(0, 32, choose_parts, 0)

    def start_fetch(n, carry):
        for copy in fetch_copies(n):
            copy.start()
        return carry

    lax.fori_loop(1, 32, start_fetch, 0)
    for copy in own_fetch:
        copy.start()

    def combine(k, carry):
        for off in range(1, 8):
            r_copy(k, off).wait_recv()
        part = jnp.dot(mix, cbuf[k].reshape(total, width), preferred_element_type=F32)
        own[k] = part[:both]
        third[k] = part[3 * both:]
        sbuf[k, 0] = part[both:2 * both].astype(BF)
        sbuf[k, 1] = part[2 * both:3 * both].astype(BF)
        for m in (1, 0):
            b_copy(k, m).start()

        @pl.when(k > 0)
        def _():
            fold(k - 1)

        return carry

    def fold(k):
        b_copy(k, 1).wait_recv()
        sbuf[k, 2] = (third[k] + gbuf[k, 1].astype(F32)).astype(BF)
        b_copy(k, 2).start()

    lax.fori_loop(0, CHUNKS, combine, 0)
    fold(CHUNKS - 1)

    kv_swap.wait()
    acc[...] = jnp.zeros_like(acc)

    def finish(k, squares):
        for m in (0, 2):
            b_copy(k, m).wait_recv()
        sums = own[k] + gbuf[k, 0].astype(F32) + gbuf[k, 2].astype(F32)
        columns = pl.ds(pl.multiple_of(k * width, width), width)
        after = (zbuf[k, 0].astype(F32) + sums).astype(BF)
        o_ref[:, columns] = after
        values = after.astype(F32)
        lines = width // 128
        gain = jnp.concatenate([gains[pl.ds(k * lines + i, 1), :] for i in range(lines)], axis=1)
        acc[...] += jnp.dot(
            (values * gain).astype(BF), kvw[columns, :], preferred_element_type=F32)
        return squares + jnp.sum(values * values, axis=1, keepdims=True)

    squares = lax.fori_loop(0, CHUNKS, finish, jnp.zeros((both, 1), F32))
    kv_ref[...] = (acc[...] * lax.rsqrt(squares / (CHUNKS * width) + 1e-06)).astype(BF)
    for n in range(1, 8):
        kv_copy(n).wait_send()
    def end_fetch(n, carry):
        for copy in spread_copies(n):
            copy.wait_send()
        for copy in fetch_copies(n):
            copy.wait_send()
            copy.wait_recv()
        return carry

    for copy in own_fetch:
        copy.wait()
    lax.fori_loop(1, 32, end_fetch, 0)
    for p in range(16):
        first, count = 8 * ((11 * p) // 2), 40 + 8 * (p % 2)
        for h in range(2):
            out_new[first:first + count, 128 * h:128 * h + 128] = fin_out[2 * p + h, :count]
    for m in range(3):
        tab_copy(m).wait_send()

    def drain(k, carry):
        for m in range(3):
            z_copy(k, m).wait_send()
            b_copy(k, m).wait_send()
        for off in range(1, 8):
            y_copy(k, off).wait_send()
            r_copy(k, off).wait_send()
        return carry

    lax.fori_loop(0, CHUNKS, drain, 0)


def routed(t1, r1, g1, t2, r2, g2, old_table, new_table, gate_up, down_proj, gain, kv_weight):
    rows, features = t1.shape
    both = 2 * rows
    inner = down_proj.shape[1]
    experts = old_table.shape[0]
    cap = 3 * rows * TOP // (2 * experts)
    slab = 8 * cap
    width = features // CHUNKS
    vmem = pl.BlockSpec(memory_space=pltpu.VMEM)
    hbm = pl.BlockSpec(memory_space=pltpu.HBM)
    dma = pltpu.SemaphoreType.DMA
    part = features // 8
    return pl.pallas_call(
        token_kernel,
        out_shape=(
            jax.ShapeDtypeStruct((both, features), BF),
            jax.ShapeDtypeStruct((both, 8 * kv_weight.shape[1]), BF),
            jax.ShapeDtypeStruct((part, 2 * inner), BF),
            jax.ShapeDtypeStruct((inner, part), BF),
        ),
        in_specs=[hbm] * 12,
        out_specs=(vmem, vmem, hbm, vmem),
        scratch_shapes=[
            pltpu.VMEM((features, 8 * kv_weight.shape[1]), BF),
            pltpu.VMEM((both, 8 * kv_weight.shape[1]), F32),
            pltpu.VMEM((features // 128, 128), BF),
            pltpu.VMEM((features // 128, 128), F32),
            pltpu.VMEM((TOP, rows), jnp.int32),
            pltpu.VMEM((TOP, rows), BF),
            pltpu.VMEM((TOP, rows), jnp.int32),
            pltpu.VMEM((TOP, rows), BF),
            pltpu.VMEM((1, 32), jnp.int32),
            pltpu.VMEM((1, 32), jnp.int32),
            pltpu.VMEM((1, 128), jnp.int32),
            pltpu.SMEM((1, 128), jnp.int32),
            pltpu.VMEM((32, 8, 2 * inner), BF),
            pltpu.VMEM((32, 48, 128), BF),
            pltpu.VMEM((32, 8, 2 * inner), BF),
            pltpu.VMEM((32, 48, 128), BF),
            pltpu.VMEM((32, 48, 128), BF),
            pltpu.VMEM((features, 2 * inner), BF),
            pltpu.VMEM((inner, features), BF),
            pltpu.VMEM((128, 128), F32),
            pltpu.VMEM((both, 128), BF),
            pltpu.VMEM((4, both, 128), BF),
            pltpu.VMEM((CHUNKS, 4, both, width), BF),
            pltpu.VMEM((CHUNKS, 8, slab, width), BF),
            pltpu.VMEM((CHUNKS, 8, slab, width), BF),
            pltpu.VMEM((8 * slab, 2 * inner), F32),
            pltpu.VMEM((CHUNKS, 8, slab, width), BF),
            pltpu.VMEM((CHUNKS, 8, slab, width), BF),
            pltpu.VMEM((CHUNKS, 3, both, width), BF),
            pltpu.VMEM((CHUNKS, 3, both, width), BF),
            pltpu.VMEM((CHUNKS, both, width), F32),
            pltpu.VMEM((CHUNKS, both, width), F32),
            dma((2,)), dma((10,)), dma((3,)), dma((3,)),
            dma((CHUNKS, 3)), dma((CHUNKS, 3)),
            dma((CHUNKS, 8)), dma((CHUNKS, 8)),
            dma((CHUNKS, 8)), dma((CHUNKS, 8)),
            dma((CHUNKS, 3)), dma((CHUNKS, 3)),
            dma((2, 32)), dma((2, 32)), dma((2, 32)), dma((2, 32)), dma((5,)), dma((8,)), dma((8,)),
        ],
        compiler_params=pltpu.CompilerParams(
            collective_id=0, has_side_effects=True, vmem_limit_bytes=60 << 20),
        cost_estimate=pl.CostEstimate(flops=8_000_000_000, bytes_accessed=200_000_000, transcendentals=0),
        name="routed_tokens",
    )(t1, r1.T, g1.T, t2, r2.T, g2.T, old_table[None, :], new_table[None, :], gate_up, down_proj,
      gain.reshape(features // 128, 128), kv_weight)


def hand_out(hid_ref, kv_ref, in_ref, out_ref, h1_ref, k1_ref, h2_ref, k2_ref, in_new, out_new, hid, kv, inv, outv, sems):
    rows = h1_ref.shape[0]
    first, second = pl.ds(0, rows), pl.ds(rows, rows)
    reads = [
        pltpu.make_async_copy(src, dst, sems.at[i])
        for i, (src, dst) in enumerate(((in_ref, inv), (out_ref, outv), (hid_ref, hid), (kv_ref, kv)))
    ]
    writes = [
        [(inv, in_new.at[0])], [(outv, out_new.at[0])],
        [(hid.at[first], h1_ref), (hid.at[second], h2_ref)], [(kv.at[first], k1_ref), (kv.at[second], k2_ref)],
    ]
    for copy in reads:
        copy.start()
    started = []
    for copy, targets in zip(reads, writes):
        copy.wait()
        for src, dst in targets:
            write = pltpu.make_async_copy(src, dst, sems.at[4 + len(started)])
            write.start()
            started.append(write)
    for write in started:
        write.wait()


def local(
    tokens_one,
    routes_one,
    gates_one,
    tokens_two,
    routes_two,
    gates_two,
    old_table,
    new_table,
    gate_up,
    down_proj,
    norm_gain,
    kv_weight,
):
    rows = tokens_one.shape[0]
    hidden, kv, in_new, out_new = routed(
        tokens_one, routes_one, gates_one, tokens_two, routes_two, gates_two, old_table, new_table,
        gate_up, down_proj, norm_gain, kv_weight)
    hbm = pl.BlockSpec(memory_space=pltpu.HBM)
    token_rows = jax.ShapeDtypeStruct((rows, hidden.shape[1]), BF)
    kv_rows = jax.ShapeDtypeStruct((rows, kv.shape[1]), BF)
    return pl.pallas_call(
        hand_out,
        out_shape=(
            token_rows, kv_rows, token_rows, kv_rows,
            jax.ShapeDtypeStruct((1,) + in_new.shape, BF), jax.ShapeDtypeStruct((1,) + out_new.shape, BF)),
        in_specs=[hbm] * 4,
        out_specs=(hbm,) * 6,
        scratch_shapes=[pltpu.VMEM(array.shape, BF) for array in (hidden, kv, in_new, out_new)]
        + [pltpu.SemaphoreType.DMA((10,))],
        compiler_params=pltpu.CompilerParams(vmem_limit_bytes=60 << 20),
        name="hand_out",
    )(hidden, kv, in_new, out_new)


def solution(mesh):
    split = P(("grp", "ep"), None)
    return jax.shard_map(
        local,
        mesh=mesh,
        in_specs=(split,) * 6 + (P(), P(), P("ep", None, None), P("ep", None, None), P(), P(None, "grp")),
        out_specs=(split,) * 4 + (P("ep", "grp", None), P("ep", None, "grp")),
        check_vma=False,
    )
```
